32 devices in a mesh: grp: 4 (over y, x), seq: 8 (over z, core).
Axes of the slice: x: 2, y: 2, z: 4, core: 2. Of those that a mesh axis runs over, the one named last changes fastest.
Arguments:
- resid_in: bfloat16 [4, 1024, 2048], P('grp', 'seq'), may hold values from -8 to 8
- lin_query: bfloat16 [4, 1024, 2048], P('grp', 'seq'), may hold values from -6 to 6
- lin_key: bfloat16 [4, 1024, 2048], P('grp', 'seq'), may hold values from -6 to 6
- lin_value: bfloat16 [4, 1024, 2048], P('grp', 'seq'), may hold values from -40 to 40
- lin_gain: float32 [2048], replicated, may hold values from 0.5 to 1.5
- out_proj: bfloat16 [2048, 2048], replicated, may hold values from -0.125 to 0.125
- moe_gain: float32 [2048], replicated, may hold values from 0.5 to 1.5
- expert_ids: int32 [4, 1024, 8], P('grp', 'seq'), may hold values from 0 to 31, all different within a row; in each aligned block of 128 rows (0 to 127, 128 to 255, ..., all dimensions but the last counted through in order) at most 40 rows name the same one
- route_scores: float32 [4, 1024, 8], P('grp', 'seq'), may hold values from 0.01 to 1
- gate_weight: bfloat16 [32, 2048, 768], P(('grp', 'seq')), may hold values from -0.125 to 0.125
- up_weight: bfloat16 [32, 2048, 768], P(('grp', 'seq')), may hold values from -0.125 to 0.125
- down_weight: bfloat16 [32, 768, 2048], P(('grp', 'seq')), may hold values from -0.875 to 0.875
Outputs:
- layer_out: bfloat16 [4, 1024, 2048], P('grp', 'seq')
The draws below stay inside these ranges and needn't reach their ends.
Inputs may be any that keep to these rules, and one draw needn't show every extreme that they name: `expert_ids`: in each aligned block of 128 rows (the rows of one device) no expert is named by more than 40 rows, a bound that some block reaches.
All inputs are finite; a program needn't handle non-finite values.
Results may differ from the reference program's by a relative error of at most 0.015.
Values may be sent and summed in bfloat16 or wider, within the bound.
No kernel may reach another device: no remote copies, remote signals or barrier semaphores. Data moves between devices by JAX's collectives and lax.ppermute only.
A program may use at most 128 MiB of HBM per device.

```python
import math
import jax
import jax.numpy as jnp
import numpy as np
from jax import lax

D = 2048
HEAD = 128
FF = 768
TOP = 8
LHEADS = 16
TOK_DEV = 128
EXPERTS = 32
SEQS = 4
SEQLEN = 1024
CAP = 40
N_SEQ = 8


def scaled_field(key, features, amplitude, limit):
    first, second, third = jax.random.split(key, 3)
    shape = (SEQS, SEQLEN, features)
    base = jax.random.normal(first, shape, jnp.float32)
    row_scale = jnp.exp(jax.random.uniform(second, (SEQS, SEQLEN, 1), jnp.float32, -1.2, 1.2))
    column_scale = jnp.exp(jax.random.uniform(third, (1, 1, features), jnp.float32, -1.2, 1.2))
    return jnp.clip(amplitude * base * row_scale * column_scale, -limit, limit).astype(jnp.bfloat16)


def draw_resid_in(key, part):
    return scaled_field(jax.random.fold_in(key, 11), D, 0.1, 8.0)


def draw_lin_value(key, part):
    return scaled_field(jax.random.fold_in(key, 23), LHEADS * HEAD, 1.0, 40.0)


def steps_of(key, extent, pieces, low, top_value):
    def one(dim, blocks):
        steps = jax.random.uniform(jax.random.fold_in(jax.random.fold_in(key, 6), dim), (blocks,), jnp.float32, low / len(pieces), top_value / len(pieces))
        return jnp.repeat(jnp.exp(steps), extent[dim] // blocks).reshape((-1,) + (1,) * (len(extent) - dim - 1))

    gain = one(*pieces[0])
    for cut in pieces[1:]:
        gain = gain * one(*cut)
    return gain


def assign_block(rng, own, number, rows, count, top, bound, lean):
    order = jax.random.permutation(rng, count)
    crowded, usual = portions_of(count, rows * top, bound, lean, True), portions_of(count, rows * top, bound, lean, False)
    places = jnp.arange(count)

    def named(tallies, rotation):
        used = int((tallies > 0).sum())
        fixed = max(1, used // 4)
        passed = fixed + (places - fixed + rotation * (used - fixed)) % max(1, count - fixed)
        return jnp.zeros((count,), jnp.int32).at[order[jnp.where(places < fixed, places, passed)]].set(jnp.asarray(tallies, jnp.int32))

    tallies = jnp.where(number % 4 == 0, named(crowded, number // 4), named(usual, number - number // 4 - 1))
    mixed = jax.random.permutation(jax.random.fold_in(own, 3), count)
    giver, taker = mixed[0:count // 2 * 2:2], mixed[1:count // 2 * 2:2]
    slack = jnp.minimum(tallies[giver] - 1, bound - tallies[taker]) // 2
    slack = jnp.where((giver == order[0]) | (taker == order[0]) | (tallies[taker] == 0), 0, jnp.maximum(slack, 0))
    passed = jax.random.randint(jax.random.fold_in(own, 4), (count // 2,), 0, 1 << 20) % (slack + 1)
    tallies = tallies.at[giver].add(-passed).at[taker].add(passed)
    items = jnp.searchsorted(jnp.cumsum(tallies), jnp.arange(rows * top), side="right").astype(jnp.int32)
    grid = items.reshape(top, rows).T
    grid = grid[jax.random.permutation(jax.random.fold_in(own, 1), rows)]
    rotation = jax.random.randint(jax.random.fold_in(own, 2), (rows, 1), 0, top)
    return jnp.take_along_axis(grid, (jnp.arange(top)[None, :] + rotation) % top, axis=1)


def portions_of(amount, total, reach, lean, full):
    weights = [(1 << 20) // math.isqrt(rank ** lean) + 1 for rank in range(1, amount + 1)]
    largest = reach if full else min(reach, max(-(-total // amount), total * weights[0] // sum(weights)))
    least = 1 if total - largest >= amount - 1 else 0
    given, rest = [largest] + [least] * (amount - 1), total - largest - least * (amount - 1)
    while rest > 0:
        movable = [i for i in range(1, amount) if given[i] < largest] or [i for i in range(1, amount) if given[i] < reach]
        whole, remaining = sum([weights[i] for i in movable]), rest
        for i in movable:
            addition = min(reach - given[i], max(1, remaining * weights[i] // whole), rest)
            given[i] = given[i] + addition
            rest = rest - addition
    return np.array(given)


def bell_draw(rng, shape, spread, reach, pieces=(), kind=jnp.bfloat16):
    values = jax.random.normal(rng, shape, jnp.float32) * spread
    if len(pieces) > 0:
        values = steps_of(rng, shape, pieces, -0.22, 0.18) * values
    return jnp.clip(values, min=-reach, max=reach).astype(kind)


def setup_inputs(seed: int = 0) -> dict:
    streams_of = jax.random.split(jax.random.key(seed), 13)
    resid_in = draw_resid_in(jax.random.fold_in(streams_of[12], 71), 0)
    lin_query = bell_draw(streams_of[1], (SEQS, SEQLEN, LHEADS * HEAD), 1.0, 6.0, ((0, 4), (1, 8)))
    lin_key = bell_draw(streams_of[2], (SEQS, SEQLEN, LHEADS * HEAD), 1.0, 6.0, ((0, 4), (1, 8)))
    lin_value = draw_lin_value(jax.random.fold_in(streams_of[12], 71), 0)
    lin_gain = jnp.clip(1.0 + 0.1 * jax.random.normal(streams_of[4], (LHEADS * HEAD,), jnp.float32), 0.5, 1.5)
    out_proj = bell_draw(streams_of[5], (LHEADS * HEAD, D), (LHEADS * HEAD) ** -0.5, 0.125)
    moe_gain = jnp.clip(1.0 + 0.1 * jax.random.normal(streams_of[6], (D,), jnp.float32), 0.5, 1.5)
    expert_ids_keys = jax.random.split(jax.random.fold_in(streams_of[7], 1), SEQS * SEQLEN // TOK_DEV)
    expert_ids_turns = jax.random.permutation(jax.random.fold_in(streams_of[7], 3), SEQS * SEQLEN // TOK_DEV)
    expert_ids = jax.vmap(lambda own, number: assign_block(jax.random.fold_in(streams_of[7], 2), own, number, TOK_DEV, EXPERTS, TOP, CAP, 2))(expert_ids_keys, expert_ids_turns).reshape((SEQS, SEQLEN, TOP))
    route_scores = jnp.clip(jnp.exp(math.log(1.0) - 4.6051702 * jax.random.uniform(streams_of[8], (SEQS, SEQLEN, TOP), jnp.float32) ** steps_of(streams_of[8], (SEQS, SEQLEN, TOP), ((0, 4), (1, 8)), -0.2, 0.2)), 0.01, 1.0)
    gate_weight = bell_draw(streams_of[9], (EXPERTS, D, FF), D ** -0.5, 0.125, ((0, 32),))
    up_weight = bell_draw(streams_of[10], (EXPERTS, D, FF), D ** -0.5, 0.125, ((0, 32),))
    down_weight = bell_draw(streams_of[11], (EXPERTS, FF, D), (FF // 16) ** -0.5, 0.875, ((0, 32),))
    return dict(resid_in=resid_in, lin_query=lin_query, lin_key=lin_key, lin_value=lin_value, lin_gain=lin_gain, out_proj=out_proj, moe_gain=moe_gain, expert_ids=expert_ids, route_scores=route_scores, gate_weight=gate_weight, up_weight=up_weight, down_weight=down_weight)


epsilon = 1e-06

def rms_norm(entries, gain_vec):
    mean_square = lax.optimization_barrier(jnp.mean(entries * entries, axis=-1, keepdims=True))
    return entries * lax.rsqrt(mean_square + epsilon) * gain_vec

def span_attend(carried, inputs):
    queries, key_rows, value_rows = inputs
    query_f = queries.astype(jnp.float32)
    key_f = key_rows.astype(jnp.float32)
    value_f = value_rows.astype(jnp.float32)
    length = queries.shape[0]
    scores = jnp.einsum('thd,shd->hts', query_f, key_f)
    causal = jnp.arange(length)[:, None] >= jnp.arange(length)[None, :]
    rounded = lax.optimization_barrier(jnp.where(causal[None], scores, 0.0).astype(jnp.bfloat16))
    inside = jnp.einsum('hts,shd->thd', rounded.astype(jnp.float32), value_f)
    carried_round = lax.optimization_barrier(carried.astype(jnp.bfloat16))
    before = jnp.einsum('thd,hde->the', query_f, carried_round.astype(jnp.float32))
    local_state = jnp.einsum('shd,she->hde', key_f, value_f)
    return (carried + local_state, inside + before)

def sequence_attend(inputs):
    shaped = tuple((tensor.reshape(N_SEQ, TOK_DEV, LHEADS, HEAD) for tensor in inputs))
    initial = jnp.zeros((LHEADS, HEAD, HEAD), jnp.float32)
    final_state, outputs = lax.scan(span_attend, initial, shaped)
    return outputs.reshape(SEQLEN, LHEADS, HEAD)

def block_slots(block_ids):
    onehot = (block_ids[:, :, None] == jnp.arange(EXPERTS, dtype=jnp.int32)[None, None, :]).astype(jnp.int32)
    counts = lax.optimization_barrier(jnp.sum(onehot, axis=1))
    before = jnp.cumsum(counts, axis=0) - counts
    return jnp.take_along_axis(before, block_ids, axis=1)

def reference(resid_in, lin_query, lin_key, lin_value, lin_gain, out_proj, moe_gain, expert_ids, route_scores, gate_weight, up_weight, down_weight):
    token_count = SEQS * SEQLEN
    attended = lax.map(sequence_attend, (lin_query, lin_key, lin_value))
    normed = rms_norm(attended, lin_gain.reshape(LHEADS, HEAD)).astype(jnp.bfloat16)
    normed = normed.reshape(token_count, LHEADS * HEAD)
    projected = jnp.dot(normed, out_proj, preferred_element_type=jnp.float32)
    residual = (resid_in.reshape(token_count, D).astype(jnp.float32) + projected).astype(jnp.bfloat16)
    moe_in = rms_norm(residual.astype(jnp.float32), moe_gain).astype(jnp.bfloat16)
    blocks = token_count // TOK_DEV
    chosen = expert_ids.reshape(blocks, TOK_DEV, TOP)
    slot_rank = lax.map(block_slots, chosen)
    column = (jnp.arange(blocks, dtype=jnp.int32)[:, None, None] * CAP + slot_rank).reshape(token_count, TOP)
    flat_ids = expert_ids.reshape(token_count, TOP)
    token_index = jnp.broadcast_to(jnp.arange(token_count, dtype=jnp.int32)[:, None], (token_count, TOP))
    weights = route_scores.reshape(token_count, TOP)
    weights = weights / lax.optimization_barrier(jnp.sum(weights, axis=1, keepdims=True))
    slot_table = jnp.full((EXPERTS, blocks * CAP), token_count, jnp.int32).at[flat_ids, column].set(token_index)
    weight_table = jnp.zeros((EXPERTS, blocks * CAP), jnp.float32).at[flat_ids, column].set(weights)
    padded = jnp.concatenate([moe_in, jnp.zeros((1, D), jnp.bfloat16)], axis=0)

    def expert_step(accumulated, inputs):
        row_index, row_weights, gate_w, up_w, down_w = inputs
        rows = padded[row_index]
        gate_act = jnp.dot(rows, gate_w, preferred_element_type=jnp.float32)
        up_act = jnp.dot(rows, up_w, preferred_element_type=jnp.float32)
        hidden = (jax.nn.silu(gate_act) * up_act).astype(jnp.bfloat16)
        result = lax.optimization_barrier(jnp.dot(hidden, down_w, preferred_element_type=jnp.float32).astype(jnp.bfloat16))
        accumulated = accumulated.at[row_index].add(row_weights[:, None] * result.astype(jnp.float32))
        return (accumulated, None)
    initial = jnp.zeros((token_count + 1, D), jnp.float32)
    accumulated, unused = lax.scan(expert_step, initial, (slot_table, weight_table, gate_weight, up_weight, down_weight))
    layer_out = (residual.astype(jnp.float32) + accumulated[:token_count]).astype(jnp.bfloat16)
    return layer_out.reshape(SEQS, SEQLEN, D)
```

```python
import functools

import jax
import jax.numpy as jnp
from jax import lax
from jax.experimental import pallas as pl
from jax.experimental.pallas import tpu as pltpu
from jax.sharding import PartitionSpec as P

HEAD = 128
TOP = 8
epsilon = 1e-06
BF = jnp.bfloat16
F32 = jnp.float32


def dot(a, b, ca=1, cb=0):
    return lax.dot_general(a, b, (((ca,), (cb,)), ((), ())), preferred_element_type=F32)


def whole(shape):
    return pl.BlockSpec(shape, lambda *_: (0,) * len(shape))


def state_kernel(k_ref, v_ref, s_ref):
    heads = k_ref.shape[1] // HEAD
    for h in range(heads):
        cols = slice(h * HEAD, (h + 1) * HEAD)
        s_ref[cols, :] = dot(k_ref[:, cols], v_ref[:, cols], 0, 0).astype(BF)


def local_states(keys, values):
    return pl.pallas_call(
        state_kernel,
        out_shape=jax.ShapeDtypeStruct((keys.shape[1], HEAD), BF),
        name="states",
    )(keys, values)


def inside_kernel(q_ref, k_ref, v_ref, o_ref):
    tokens = q_ref.shape[0]
    heads = q_ref.shape[1] // HEAD
    rows = lax.broadcasted_iota(jnp.int32, (tokens, tokens), 0)
    cols = lax.broadcasted_iota(jnp.int32, (tokens, tokens), 1)
    causal = rows >= cols
    for h in range(heads):
        part = slice(h * HEAD, (h + 1) * HEAD)
        scores = dot(q_ref[:, part], k_ref[:, part], 1, 1)
        scores = jnp.where(causal, scores, 0.0).astype(BF)
        o_ref[:, part] = dot(scores, v_ref[:, part])


def inside_block(queries, keys, values):
    return pl.pallas_call(
        inside_kernel,
        out_shape=jax.ShapeDtypeStruct(queries.shape, F32),
        name="inside",
    )(queries, keys, values)


def project_kernel(
    core_ref, in_ref, q_ref, mine_ref, other_ref, pair_ref, gain_ref, resid_ref, w_ref, mgain_ref,
    res_ref, moe_ref, normed_ref, square_ref,
):
    step = pl.program_id(0)
    core = core_ref[0]
    heads = q_ref.shape[1] // HEAD
    half = heads // 2

    @pl.when(step == 0)
    def _():
        low = core == 0
        second = jnp.where(low, 0.0, 1.0)
        for h in range(heads):
            part = slice(h * HEAD, (h + 1) * HEAD)
            at = slice((h % half) * HEAD, (h % half + 1) * HEAD)
            first = low if h < half else jnp.logical_not(low)
            prefix = jnp.where(first, mine_ref[at, :].astype(F32), other_ref[at, :].astype(F32))
            carried = (prefix + second * pair_ref[part, :].astype(F32)).astype(BF)
            attended = in_ref[:, part] + dot(q_ref[:, part], carried)
            mean = jnp.mean(attended * attended, axis=1, keepdims=True)
            normed_ref[:, part] = (
                attended * lax.rsqrt(mean + epsilon) * gain_ref[:, part]
            ).astype(BF)
        square_ref[...] = jnp.zeros_like(square_ref)

    width = w_ref.shape[1]
    at = pl.ds(pl.multiple_of(step * width, width), width)
    added = resid_ref[:, at].astype(F32) + dot(normed_ref[...], w_ref[...])
    rounded = added.astype(BF)
    res_ref[:, at] = rounded
    wide = rounded.astype(F32)
    square_ref[...] += jnp.sum(wide * wide, axis=1, keepdims=True)

    @pl.when(step == pl.num_programs(0) - 1)
    def _():
        features = res_ref.shape[1]
        scale = lax.rsqrt(square_ref[...] / features + epsilon)
        moe_ref[...] = (res_ref[...].astype(F32) * scale * mgain_ref[...]).astype(BF)


def attend_project(core, inside, queries, mine, other, pair, gain, resid, weight, moe_gain):
    tokens, features = resid.shape
    inner = queries.shape[1]
    steps = 4
    width = features // steps
    return pl.pallas_call(
        project_kernel,
        grid_spec=pltpu.PrefetchScalarGridSpec(
            num_scalar_prefetch=1,
            grid=(steps,),
            in_specs=[
                whole(inside.shape), whole(queries.shape), whole(mine.shape), whole(other.shape),
                whole(pair.shape), whole(gain.shape), whole(resid.shape),
                pl.BlockSpec((inner, width), lambda i, *_: (0, i)),
                whole(moe_gain.shape),
            ],
            out_specs=[whole(resid.shape), whole(resid.shape)],
            scratch_shapes=[pltpu.VMEM((tokens, inner), BF), pltpu.VMEM((tokens, 1), F32)],
        ),
        out_shape=[jax.ShapeDtypeStruct(resid.shape, BF)] * 2,
        compiler_params=pltpu.CompilerParams(dimension_semantics=("arbitrary",)),
        name="project",
    )(core, inside, queries, mine, other, pair, gain, resid, weight, moe_gain)


def slots_of(rank_ref, weight_ref, row, slots, weighted):
    rank = rank_ref[row : row + 1, :]
    weight = weight_ref[row : row + 1, :]
    number = lax.broadcasted_iota(jnp.int32, (slots, rank.shape[1]), 0).astype(F32)
    hit = jnp.logical_and(number == rank, weight > 0.0)
    return jnp.where(hit, weight if weighted else 1.0, 0.0)


def select_kernel(slots, own_ref, par_ref, rank_ref, weight_ref, *outs):
    groups = len(outs)
    picks = []
    for block in range(2):
        rows = [
            slots_of(rank_ref, weight_ref, block * groups + k, slots, False) for k in range(groups)
        ]
        picks.append(jnp.concatenate(rows, axis=0).astype(BF))
    first = dot(picks[0], own_ref[...])
    second = dot(picks[1], par_ref[...])
    for k in range(groups):
        at = slice(k * slots, (k + 1) * slots)
        outs[k][...] = jnp.concatenate([first[at], second[at]], axis=0).astype(BF)


def select(slots, groups, own, par, rank, weight):
    shape = jax.ShapeDtypeStruct((2 * slots, own.shape[1]), BF)
    return pl.pallas_call(
        functools.partial(select_kernel, slots), out_shape=[shape] * groups, name="select"
    )(own, par, rank, weight)


def combine_kernel(slots, groups, *refs):
    backs = refs[:groups]
    rank_ref, weight_ref, own_ref, par_ref = refs[groups:]
    rows = jnp.concatenate([r[...] for r in backs], axis=0)
    zero = jnp.zeros((slots, rank_ref.shape[1]), F32)
    sides = []
    for block in range(2):
        parts = []
        for k in range(groups):
            mine = slots_of(rank_ref, weight_ref, block * groups + k, slots, True)
            parts += [mine, zero] if block == 0 else [zero, mine]
        sides.append(jnp.concatenate(parts, axis=0).astype(BF))
    own_ref[...] = dot(sides[0], rows, 0, 0).astype(BF)
    par_ref[...] = dot(sides[1], rows, 0, 0).astype(BF)


def combine(slots, backs, rank, weight):
    tokens = rank.shape[1]
    shape = jax.ShapeDtypeStruct((tokens, backs[0].shape[1]), BF)
    return pl.pallas_call(
        functools.partial(combine_kernel, slots, len(backs)), out_shape=[shape] * 2, name="combine"
    )(*backs, rank, weight)


def expert_kernel(groups, *refs):
    xs = refs[:groups]
    gate_ref, up_ref, down_ref = refs[groups : groups + 3]
    outs = refs[groups + 3 : 2 * groups + 3]
    x_ref, acc_ref = refs[2 * groups + 3 :]
    step = pl.program_id(0)
    rows = xs[0].shape[0]

    @pl.when(step == 0)
    def _():
        for k in range(groups):
            x_ref[k * rows : (k + 1) * rows, :] = xs[k][...]

    x = x_ref[...]
    gate = dot(x, gate_ref[0])
    up = dot(x, up_ref[0])
    hidden = (gate / (1.0 + jnp.exp(-gate)) * up).astype(BF)
    out = dot(hidden, down_ref[0])

    @pl.when(step == 0)
    def _():
        acc_ref[...] = out

    @pl.when(jnp.logical_and(step > 0, step < pl.num_programs(0) - 1))
    def _():
        acc_ref[...] += out

    @pl.when(step == pl.num_programs(0) - 1)
    def _():
        for k in range(groups):
            at = slice(k * rows, (k + 1) * rows)
            outs[k][...] = (acc_ref[at, :] + out[at, :]).astype(BF)


def experts(xs, gate, up, down):
    groups = len(xs)
    rows, features = xs[0].shape
    width = 256
    steps = gate.shape[2] // width
    return pl.pallas_call(
        functools.partial(expert_kernel, groups),
        grid=(steps,),
        in_specs=[whole(xs[0].shape)] * groups
        + [
            pl.BlockSpec((1, features, width), lambda i: (0, 0, i)),
            pl.BlockSpec((1, features, width), lambda i: (0, 0, i)),
            pl.BlockSpec((1, width, features), lambda i: (0, i, 0)),
        ],
        out_specs=[whole(xs[0].shape)] * groups,
        out_shape=[jax.ShapeDtypeStruct(xs[0].shape, BF)] * groups,
        scratch_shapes=[
            pltpu.VMEM((groups * rows, features), BF),
            pltpu.VMEM((groups * rows, features), F32),
        ],
        compiler_params=pltpu.CompilerParams(dimension_semantics=("arbitrary",)),
        name="experts",
    )(*xs, gate, up, down)


def on_device(
    resid_in,
    lin_query,
    lin_key,
    lin_value,
    lin_gain,
    out_proj,
    moe_gain,
    expert_ids,
    route_scores,
    gate_weight,
    up_weight,
    down_weight,
):
    tokens = resid_in.shape[1]
    features = resid_in.shape[2]
    groups = lax.axis_size("grp")
    length = lax.axis_size("seq")
    stages = length // 2
    group = lax.axis_index("grp")
    place = lax.axis_index("seq")
    core = place % 2
    expert_count = gate_weight.shape[0] * groups * length
    capacity = tokens * TOP * 5 // (4 * expert_count)
    slots = -(-capacity // 8) * 8

    def swap(x):
        return lax.ppermute(x, "seq", [(s, s ^ 1) for s in range(length)])

    def along(x, m):
        return lax.ppermute(x, "seq", [(s, s ^ (2 * m)) for s in range(length)])

    def across(x, m):
        if m == 0:
            return x
        return lax.ppermute(x, "grp", [(g, g ^ m) for g in range(groups)])

    def later(x, m):
        return lax.ppermute(x, "seq", [(s, s + 2 * m) for s in range(length - 2 * m)])

    queries = lin_query.reshape(tokens, -1)
    keys = lin_key.reshape(tokens, -1)
    values = lin_value.reshape(tokens, -1)
    inner = queries.shape[1]
    half = inner // 2

    states = local_states(keys, values)
    pair = swap(states)
    summed = (states.astype(F32) + pair.astype(F32)).astype(BF)
    summed = lax.dynamic_slice_in_dim(summed, core * half, half, axis=0)
    arrived = [later(summed, m) for m in range(1, stages)]

    chosen = expert_ids.reshape(tokens, TOP).T
    scores = route_scores.reshape(tokens, TOP)
    shares = (scores / jnp.sum(scores, axis=1, keepdims=True)).T
    named = chosen[None] == jnp.arange(expert_count, dtype=jnp.int32)[:, None, None]
    dense = jnp.sum(jnp.where(named, shares[None], 0.0), axis=1)
    both = jnp.stack([dense, swap(dense)])
    routes = jnp.stack([both] + [along(both, m) for m in range(1, stages)])
    routes = routes.reshape(stages, 2, groups, length, tokens)
    routes = lax.dynamic_index_in_dim(routes, place, axis=3, keepdims=False)
    routes = jnp.stack(
        [
            lax.dynamic_index_in_dim(routes, group ^ k, axis=2, keepdims=False)
            for k in range(groups)
        ],
        axis=2,
    ).reshape(stages, 2 * groups, tokens)
    earlier = (jnp.arange(tokens)[:, None] < jnp.arange(tokens)[None, :]).astype(BF)
    ranks = jnp.einsum(
        "srt,tu->sru", (routes > 0.0).astype(BF), earlier, preferred_element_type=F32
    )

    inside = inside_block(queries, keys, values)
    total = arrived[0].astype(F32)
    for more in arrived[1:]:
        total = total + more.astype(F32)
    mine = total.astype(BF)
    other = swap(mine)
    residual, moe_in = attend_project(
        core.reshape(1),
        inside,
        queries,
        mine,
        other,
        pair,
        lin_gain.reshape(1, inner),
        resid_in.reshape(tokens, features),
        out_proj,
        moe_gain.reshape(1, features),
    )

    order = [0, 1] + list(range(stages - 1, 1, -1))
    blocks = {0: moe_in}
    for m in order[1:]:
        blocks[m] = along(moe_in, m)
    outs = {}
    for m in order:
        picked = select(slots, groups, blocks[m], swap(blocks[m]), ranks[m], routes[m])
        taken = [across(picked[k], k) for k in range(groups)]
        outs[m] = experts(taken, gate_weight, up_weight, down_weight)
    combined = residual.astype(F32)
    for m in order[2:] + [1, 0]:
        backs = [across(outs[m][k], k) for k in range(groups)]
        own, par = combine(slots, backs, ranks[m], routes[m])
        part = own.astype(F32) + swap(par).astype(F32)
        if m:
            part = along(part.astype(BF), m).astype(F32)
        combined = combined + part
    return combined.astype(BF).reshape(1, tokens, features)


def solution(mesh):
    rows = P("grp", "seq", None)
    held = P(("grp", "seq"), None, None)
    in_specs = (rows, rows, rows, rows, P(), P(), P(), rows, rows, held, held, held)
    return jax.shard_map(
        on_device, mesh=mesh, in_specs=in_specs, out_specs=rows, check_vma=False
    )
```

```python
import functools

import jax
import jax.numpy as jnp
from jax import lax
from jax.experimental import pallas as pl
from jax.experimental.pallas import tpu as pltpu
from jax.sharding import PartitionSpec as P


HEAD = 128
TOP = 8
epsilon = 1e-06
BF = jnp.bfloat16
F32 = jnp.float32


def dot(a, b, ca=1, cb=0):
    return lax.dot_general(a, b, (((ca,), (cb,)), ((), ())), preferred_element_type=F32)


def whole(shape):
    return pl.BlockSpec(shape, lambda *_: (0,) * len(shape))


def state_kernel(k_ref, v_ref, s_ref):
    heads = k_ref.shape[1] // HEAD
    for h in range(heads):
        cols = slice(h * HEAD, (h + 1) * HEAD)
        s_ref[cols, :] = dot(k_ref[:, cols], v_ref[:, cols], 0, 0).astype(BF)


def local_states(keys, values):
    return pl.pallas_call(
        state_kernel,
        out_shape=jax.ShapeDtypeStruct((keys.shape[1], HEAD), BF),
        name="states",
    )(keys, values)


def inside_kernel(q_ref, k_ref, v_ref, o_ref):
    tokens = q_ref.shape[0]
    heads = q_ref.shape[1] // HEAD
    rows = lax.broadcasted_iota(jnp.int32, (tokens, tokens), 0)
    cols = lax.broadcasted_iota(jnp.int32, (tokens, tokens), 1)
    causal = rows >= cols
    for h in range(heads):
        part = slice(h * HEAD, (h + 1) * HEAD)
        scores = dot(q_ref[:, part], k_ref[:, part], 1, 1)
        scores = jnp.where(causal, scores, 0.0).astype(BF)
        o_ref[:, part] = dot(scores, v_ref[:, part])


def inside_block(queries, keys, values):
    return pl.pallas_call(
        inside_kernel,
        out_shape=jax.ShapeDtypeStruct(queries.shape, F32),
        name="inside",
    )(queries, keys, values)


def project_kernel(
    core_ref, in_ref, q_ref, mine_ref, other_ref, pair_ref, gain_ref, resid_ref, w_ref, mgain_ref,
    res_ref, moe_ref, normed_ref, square_ref,
):
    step = pl.program_id(0)
    core = core_ref[0]
    heads = q_ref.shape[1] // HEAD
    half = heads // 2

    @pl.when(step == 0)
    def _():
        low = core == 0
        second = jnp.where(low, 0.0, 1.0)
        for h in range(heads):
            part = slice(h * HEAD, (h + 1) * HEAD)
            at = slice((h % half) * HEAD, (h % half + 1) * HEAD)
            first = low if h < half else jnp.logical_not(low)
            prefix = jnp.where(first, mine_ref[at, :].astype(F32), other_ref[at, :].astype(F32))
            carried = (prefix + second * pair_ref[part, :].astype(F32)).astype(BF)
            attended = in_ref[:, part] + dot(q_ref[:, part], carried)
            mean = jnp.mean(attended * attended, axis=1, keepdims=True)
            normed_ref[:, part] = (
                attended * lax.rsqrt(mean + epsilon) * gain_ref[:, part]
            ).astype(BF)
        square_ref[...] = jnp.zeros_like(square_ref)

    width = w_ref.shape[1]
    at = pl.ds(pl.multiple_of(step * width, width), width)
    added = resid_ref[:, at].astype(F32) + dot(normed_ref[...], w_ref[...])
    rounded = added.astype(BF)
    res_ref[:, at] = rounded
    wide = rounded.astype(F32)
    square_ref[...] += jnp.sum(wide * wide, axis=1, keepdims=True)

    @pl.when(step == pl.num_programs(0) - 1)
    def _():
        features = res_ref.shape[1]
        scale = lax.rsqrt(square_ref[...] / features + epsilon)
        moe_ref[...] = (res_ref[...].astype(F32) * scale * mgain_ref[...]).astype(BF)


def attend_project(core, inside, queries, mine, other, pair, gain, resid, weight, moe_gain):
    tokens, features = resid.shape
    inner = queries.shape[1]
    steps = 4
    width = features // steps
    return pl.pallas_call(
        project_kernel,
        grid_spec=pltpu.PrefetchScalarGridSpec(
            num_scalar_prefetch=1,
            grid=(steps,),
            in_specs=[
                whole(inside.shape), whole(queries.shape), whole(mine.shape), whole(other.shape),
                whole(pair.shape), whole(gain.shape), whole(resid.shape),
                pl.BlockSpec((inner, width), lambda i, *_: (0, i)),
                whole(moe_gain.shape),
            ],
            out_specs=[whole(resid.shape), whole(resid.shape)],
            scratch_shapes=[pltpu.VMEM((tokens, inner), BF), pltpu.VMEM((tokens, 1), F32)],
        ),
        out_shape=[jax.ShapeDtypeStruct(resid.shape, BF)] * 2,
        compiler_params=pltpu.CompilerParams(dimension_semantics=("arbitrary",)),
        name="project",
    )(core, inside, queries, mine, other, pair, gain, resid, weight, moe_gain)


def slots_of(rank_ref, weight_ref, row, slots, weighted):
    rank = rank_ref[row : row + 1, :]
    weight = weight_ref[row : row + 1, :]
    number = lax.broadcasted_iota(jnp.int32, (slots, rank.shape[1]), 0).astype(F32)
    hit = jnp.logical_and(number == rank, weight > 0.0)
    return jnp.where(hit, weight if weighted else 1.0, 0.0)


def select_kernel(slots, own_ref, par_ref, rank_ref, weight_ref, *outs):
    groups = len(outs)
    picks = []
    for block in range(2):
        rows = [
            slots_of(rank_ref, weight_ref, block * groups + k, slots, False) for k in range(groups)
        ]
        picks.append(jnp.concatenate(rows, axis=0).astype(BF))
    first = dot(picks[0], own_ref[...])
    second = dot(picks[1], par_ref[...])
    for k in range(groups):
        at = slice(k * slots, (k + 1) * slots)
        outs[k][...] = jnp.concatenate([first[at], second[at]], axis=0).astype(BF)


def select(slots, groups, own, par, rank, weight):
    shape = jax.ShapeDtypeStruct((2 * slots, own.shape[1]), BF)
    return pl.pallas_call(
        functools.partial(select_kernel, slots), out_shape=[shape] * groups, name="select"
    )(own, par, rank, weight)


def combine_kernel(slots, groups, *refs):
    backs = refs[:groups]
    rank_ref, weight_ref, own_ref, par_ref = refs[groups:]
    rows = jnp.concatenate([r[...] for r in backs], axis=0)
    zero = jnp.zeros((slots, rank_ref.shape[1]), F32)
    sides = []
    for block in range(2):
        parts = []
        for k in range(groups):
            mine = slots_of(rank_ref, weight_ref, block * groups + k, slots, True)
            parts += [mine, zero] if block == 0 else [zero, mine]
        sides.append(jnp.concatenate(parts, axis=0).astype(BF))
    own_ref[...] = dot(sides[0], rows, 0, 0).astype(BF)
    par_ref[...] = dot(sides[1], rows, 0, 0).astype(BF)


def combine(slots, backs, rank, weight):
    tokens = rank.shape[1]
    shape = jax.ShapeDtypeStruct((tokens, backs[0].shape[1]), BF)
    return pl.pallas_call(
        functools.partial(combine_kernel, slots, len(backs)), out_shape=[shape] * 2, name="combine"
    )(*backs, rank, weight)


def expert_kernel(groups, *refs):
    xs = refs[:groups]
    gate_ref, up_ref, down_ref = refs[groups : groups + 3]
    outs = refs[groups + 3 : 2 * groups + 3]
    x_ref, acc_ref = refs[2 * groups + 3 :]
    step = pl.program_id(0)
    rows = xs[0].shape[0]

    @pl.when(step == 0)
    def _():
        for k in range(groups):
            x_ref[k * rows : (k + 1) * rows, :] = xs[k][...]

    x = x_ref[...]
    gate = dot(x, gate_ref[0])
    up = dot(x, up_ref[0])
    hidden = (gate / (1.0 + jnp.exp(-gate)) * up).astype(BF)
    out = dot(hidden, down_ref[0])

    @pl.when(step == 0)
    def _():
        acc_ref[...] = out

    @pl.when(jnp.logical_and(step > 0, step < pl.num_programs(0) - 1))
    def _():
        acc_ref[...] += out

    @pl.when(step == pl.num_programs(0) - 1)
    def _():
        for k in range(groups):
            at = slice(k * rows, (k + 1) * rows)
            outs[k][...] = (acc_ref[at, :] + out[at, :]).astype(BF)


def experts(xs, gate, up, down):
    groups = len(xs)
    rows, features = xs[0].shape
    width = 256
    steps = gate.shape[2] // width
    return pl.pallas_call(
        functools.partial(expert_kernel, groups),
        grid=(steps,),
        in_specs=[whole(xs[0].shape)] * groups
        + [
            pl.BlockSpec((1, features, width), lambda i: (0, 0, i)),
            pl.BlockSpec((1, features, width), lambda i: (0, 0, i)),
            pl.BlockSpec((1, width, features), lambda i: (0, i, 0)),
        ],
        out_specs=[whole(xs[0].shape)] * groups,
        out_shape=[jax.ShapeDtypeStruct(xs[0].shape, BF)] * groups,
        scratch_shapes=[
            pltpu.VMEM((groups * rows, features), BF),
            pltpu.VMEM((groups * rows, features), F32),
        ],
        compiler_params=pltpu.CompilerParams(dimension_semantics=("arbitrary",)),
        name="experts",
    )(*xs, gate, up, down)


def on_device(
    resid_in,
    lin_query,
    lin_key,
    lin_value,
    lin_gain,
    out_proj,
    moe_gain,
    expert_ids,
    route_scores,
    gate_weight,
    up_weight,
    down_weight,
):
    tokens = resid_in.shape[1]
    features = resid_in.shape[2]
    groups = lax.axis_size("grp")
    length = lax.axis_size("seq")
    stages = length // 2
    group = lax.axis_index("grp")
    place = lax.axis_index("seq")
    core = place % 2
    expert_count = gate_weight.shape[0] * groups * length
    capacity = tokens * TOP * 5 // (4 * expert_count)
    slots = -(-capacity // 8) * 8

    def swap(x):
        return lax.ppermute(x, "seq", [(s, s ^ 1) for s in range(length)])

    def along(x, m):
        return lax.ppermute(x, "seq", [(s, s ^ (2 * m)) for s in range(length)])

    def across(x, m):
        if m == 0:
            return x
        return lax.ppermute(x, "grp", [(g, g ^ m) for g in range(groups)])

    def later(x, m):
        return lax.ppermute(x, "seq", [(s, s + 2 * m) for s in range(length - 2 * m)])

    queries = lin_query.reshape(tokens, -1)
    keys = lin_key.reshape(tokens, -1)
    values = lin_value.reshape(tokens, -1)
    inner = queries.shape[1]
    half = inner // 2

    states = local_states(keys, values)
    pair = swap(states)
    summed = (states.astype(F32) + pair.astype(F32)).astype(BF)
    summed = lax.dynamic_slice_in_dim(summed, core * half, half, axis=0)
    arrived = [later(summed, m) for m in range(1, stages)]

    chosen = expert_ids.reshape(tokens, TOP).T
    scores = route_scores.reshape(tokens, TOP)
    shares = (scores / jnp.sum(scores, axis=1, keepdims=True)).T
    hit = chosen[None] == jnp.arange(expert_count, dtype=jnp.int32)[:, None, None]
    dense = jnp.sum(jnp.where(hit, shares[None], 0.0), axis=1)
    both = jnp.stack([dense, swap(dense)])
    routes = jnp.stack([both] + [along(both, m) for m in range(1, stages)])
    routes = routes.reshape(stages, 2, groups, length, tokens)
    routes = lax.dynamic_index_in_dim(routes, place, axis=3, keepdims=False)
    routes = jnp.stack(
        [
            lax.dynamic_index_in_dim(routes, group ^ k, axis=2, keepdims=False)
            for k in range(groups)
        ],
        axis=2,
    ).reshape(stages, 2 * groups, tokens)
    earlier = (jnp.arange(tokens)[:, None] < jnp.arange(tokens)[None, :]).astype(BF)
    ranks = jnp.einsum(
        "srt,tu->sru", (routes > 0.0).astype(BF), earlier, preferred_element_type=F32
    )

    inside = inside_block(queries, keys, values)
    total = arrived[0].astype(F32)
    for more in arrived[1:]:
        total = total + more.astype(F32)
    mine = total.astype(BF)
    other = swap(mine)
    residual, moe_in = attend_project(
        core.reshape(1),
        inside,
        queries,
        mine,
        other,
        pair,
        lin_gain.reshape(1, inner),
        resid_in.reshape(tokens, features),
        out_proj,
        moe_gain.reshape(1, features),
    )

    order = visits(stages)
    blocks = {0: moe_in}
    for m in order[1:]:
        blocks[m] = along(moe_in, m)
    outs = {}
    for m in order:
        partner = swap(blocks[m])
        picked = select(slots, groups, blocks[m], partner, ranks[m], routes[m])
        taken = [across(picked[k], k) for k in range(groups)]
        outs[m] = experts(taken, gate_weight, up_weight, down_weight)
    combined = residual.astype(F32)
    for m in order[2:] + [1, 0]:
        backs = [across(outs[m][k], k) for k in range(groups)]
        own, par = combine(slots, backs, ranks[m], routes[m])
        part = own.astype(F32) + swap(par).astype(F32)
        if m:
            part = along(part.astype(BF), m).astype(F32)
        combined = combined + part
    return combined.astype(BF).reshape(1, tokens, features)


def visits(stages):
    return [0, 1] + list(range(stages - 1, 1, -1))


def solution(mesh):
    rows = P("grp", "seq", None)
    held = P(("grp", "seq"), None, None)
    in_specs = (rows, rows, rows, rows, P(), P(), P(), rows, rows, held, held, held)

    return jax.shard_map(on_device, mesh=mesh, in_specs=in_specs, out_specs=rows, check_vma=False)
```

```python
import functools

import jax
import jax.numpy as jnp
from jax import lax
from jax.experimental import pallas as pl
from jax.experimental.pallas import tpu as pltpu
from jax.sharding import PartitionSpec as P


HEAD = 128
TOP = 8
epsilon = 1e-06
BF = jnp.bfloat16
F32 = jnp.float32


def dot(a, b, ca=1, cb=0):
    return lax.dot_general(a, b, (((ca,), (cb,)), ((), ())), preferred_element_type=F32)


def call(body, outs, scratch=(), limit=24):
    def run(*args):
        specs = []
        placed = []
        for x in args:
            space = pltpu.SMEM if x.size == 1 else pltpu.VMEM
            specs.append(pl.BlockSpec(memory_space=space))
            placed.append(pltpu.with_memory_space_constraint(x, space))
        return pl.pallas_call(
            body,
            in_specs=specs,
            out_specs=[pl.BlockSpec(memory_space=pltpu.VMEM)] * len(outs),
            out_shape=[pltpu.VMEM(shape, dtype) for shape, dtype in outs],
            scratch_shapes=list(scratch),
            compiler_params=pltpu.CompilerParams(vmem_limit_bytes=limit << 20),
        )(*placed)

    return run


def state_kernel(k_ref, v_ref, s_ref):
    heads = k_ref.shape[1] // HEAD
    for h in range(heads):
        cols = slice(h * HEAD, (h + 1) * HEAD)
        s_ref[cols, :] = dot(k_ref[:, cols], v_ref[:, cols], 0, 0).astype(BF)


def inside_kernel(q_ref, k_ref, v_ref, o_ref):
    tokens = q_ref.shape[0]
    heads = q_ref.shape[1] // HEAD
    rows = lax.broadcasted_iota(jnp.int32, (tokens, tokens), 0)
    cols = lax.broadcasted_iota(jnp.int32, (tokens, tokens), 1)
    causal = rows >= cols
    for h in range(heads):
        part = slice(h * HEAD, (h + 1) * HEAD)
        scores = dot(q_ref[:, part], k_ref[:, part], 1, 1)
        scores = jnp.where(causal, scores, 0.0).astype(BF)
        o_ref[:, part] = dot(scores, v_ref[:, part])


def project_kernel(
    core_ref, in_ref, q_ref, mine_ref, other_ref, pair_ref, gain_ref, resid_ref, w_ref, mgain_ref,
    res_ref, moe_ref, normed_ref,
):
    core = core_ref[0]
    heads = q_ref.shape[1] // HEAD
    half = heads // 2
    low = core == 0
    second = jnp.where(low, 0.0, 1.0)
    for h in range(heads):
        part = slice(h * HEAD, (h + 1) * HEAD)
        at = slice((h % half) * HEAD, (h % half + 1) * HEAD)
        first = low if h < half else jnp.logical_not(low)
        prefix = jnp.where(first, mine_ref[at, :].astype(F32), other_ref[at, :].astype(F32))
        carried = (prefix + second * pair_ref[part, :].astype(F32)).astype(BF)
        attended = in_ref[:, part] + dot(q_ref[:, part], carried)
        mean = jnp.mean(attended * attended, axis=1, keepdims=True)
        normed_ref[:, part] = (attended * lax.rsqrt(mean + epsilon) * gain_ref[:, part]).astype(BF)
    features = res_ref.shape[1]
    width = features // 4
    square = jnp.zeros((res_ref.shape[0], 1), F32)
    for i in range(4):
        at = slice(i * width, (i + 1) * width)
        added = resid_ref[:, at].astype(F32) + dot(normed_ref[...], w_ref[:, at])
        rounded = added.astype(BF)
        res_ref[:, at] = rounded
        wide = rounded.astype(F32)
        square = square + jnp.sum(wide * wide, axis=1, keepdims=True)
    scale = lax.rsqrt(square / features + epsilon)
    moe_ref[...] = (res_ref[...].astype(F32) * scale * mgain_ref[...]).astype(BF)


def rank_kernel(route_ref, rank_ref):
    tokens = route_ref.shape[1]
    rows = lax.broadcasted_iota(jnp.int32, (tokens, tokens), 0)
    cols = lax.broadcasted_iota(jnp.int32, (tokens, tokens), 1)
    earlier = jnp.where(rows < cols, 1.0, 0.0).astype(BF)
    named = route_ref[...] > 0.0
    rank = dot(jnp.where(named, 1.0, 0.0).astype(BF), earlier)
    rank_ref[...] = jnp.where(named, rank, -1.0)


def slots_of(rank_ref, value, row, slots):
    rank = rank_ref[row : row + 1, :]
    number = lax.broadcasted_iota(jnp.int32, (slots, rank.shape[1]), 0).astype(F32)
    return jnp.where(number == rank, value, 0.0)


def select_kernel(slots, base, own_ref, par_ref, rank_ref, *outs):
    groups = len(outs)
    picks = []
    for block in range(2):
        rows = [slots_of(rank_ref, 1.0, base + block * groups + k, slots) for k in range(groups)]
        picks.append(jnp.concatenate(rows, axis=0).astype(BF))
    first = dot(picks[0], own_ref[...])
    second = dot(picks[1], par_ref[...])
    for k in range(groups):
        at = slice(k * slots, (k + 1) * slots)
        outs[k][...] = jnp.concatenate([first[at], second[at]], axis=0).astype(BF)


def select(slots, groups, base, own, par, rank):
    shape = ((2 * slots, own.shape[1]), BF)
    body = functools.partial(select_kernel, slots, base)
    return call(body, [shape] * groups)(own, par, rank)


def combine_kernel(slots, groups, base, *refs):
    backs = refs[:groups]
    rank_ref, weight_ref, own_ref, par_ref = refs[groups:]
    rows = jnp.concatenate([r[...] for r in backs], axis=0)
    zero = jnp.zeros((slots, rank_ref.shape[1]), F32)
    sides = []
    for block in range(2):
        parts = []
        for k in range(groups):
            row = base + block * groups + k
            mine = slots_of(rank_ref, weight_ref[row : row + 1, :], row, slots)
            parts += [mine, zero] if block == 0 else [zero, mine]
        sides.append(jnp.concatenate(parts, axis=0).astype(BF))
    own_ref[...] = dot(sides[0], rows, 0, 0).astype(BF)
    par_ref[...] = dot(sides[1], rows, 0, 0).astype(BF)


def combine(slots, base, backs, rank, weight):
    shape = ((rank.shape[1], backs[0].shape[1]), BF)
    body = functools.partial(combine_kernel, slots, len(backs), base)
    return call(body, [shape] * 2)(*backs, rank, weight)


def expert_kernel(groups, *refs):
    xs = refs[:groups]
    gate_ref, up_ref, down_ref = refs[groups : groups + 3]
    outs = refs[groups + 3 : 2 * groups + 3]
    hidden_ref = refs[2 * groups + 3]
    rows, features = xs[0].shape
    units = gate_ref.shape[2]
    x = jnp.concatenate([r[...] for r in xs], axis=0)
    width = 256
    for j in range(units // width):
        at = slice(j * width, (j + 1) * width)
        gate = dot(x, gate_ref[0, :, at])
        up = dot(x, up_ref[0, :, at])
        hidden_ref[:, at] = (gate / (1.0 + jnp.exp(-gate)) * up).astype(BF)
    hidden = hidden_ref[...]
    width = 512
    for j in range(features // width):
        at = slice(j * width, (j + 1) * width)
        out = dot(hidden, down_ref[0, :, at]).astype(BF)
        for k in range(groups):
            outs[k][:, at] = out[k * rows : (k + 1) * rows]


def experts(xs, gate, up, down):
    groups = len(xs)
    body = functools.partial(expert_kernel, groups)
    scratch = [pltpu.VMEM((groups * xs[0].shape[0], gate.shape[2]), BF)]
    outs = [(xs[0].shape, BF)] * groups
    return call(body, outs, scratch)(*xs, gate, up, down)


def on_device(
    resid_in,
    lin_query,
    lin_key,
    lin_value,
    lin_gain,
    out_proj,
    moe_gain,
    expert_ids,
    route_scores,
    gate_weight,
    up_weight,
    down_weight,
):
    tokens = resid_in.shape[1]
    features = resid_in.shape[2]
    groups = lax.axis_size("grp")
    length = lax.axis_size("seq")
    stages = length // 2
    group = lax.axis_index("grp")
    place = lax.axis_index("seq")
    core = place % 2
    expert_count = gate_weight.shape[0] * groups * length
    capacity = tokens * TOP * 5 // (4 * expert_count)
    slots = -(-capacity // 8) * 8

    def swap(x):
        return lax.ppermute(x, "seq", [(s, s ^ 1) for s in range(length)])

    def along(x, m):
        return lax.ppermute(x, "seq", [(s, s ^ (2 * m)) for s in range(length)])

    def across(x, m):
        if m == 0:
            return x
        return lax.ppermute(x, "grp", [(g, g ^ m) for g in range(groups)])

    def later(x, m):
        return lax.ppermute(x, "seq", [(s, s + 2 * m) for s in range(length - 2 * m)])

    queries = lin_query.reshape(tokens, -1)
    keys = lin_key.reshape(tokens, -1)
    values = lin_value.reshape(tokens, -1)
    inner = queries.shape[1]
    half = inner // 2

    states = call(state_kernel, [((inner, HEAD), BF)])(keys, values)[0]
    pair = swap(states)
    summed = (states.astype(F32) + pair.astype(F32)).astype(BF)
    summed = lax.dynamic_slice_in_dim(summed, core * half, half, axis=0)
    arrived = [later(summed, m) for m in range(1, stages)]

    chosen = expert_ids.reshape(tokens, TOP).T
    scores = route_scores.reshape(tokens, TOP)
    shares = (scores / jnp.sum(scores, axis=1, keepdims=True)).T
    hit = chosen[None] == jnp.arange(expert_count, dtype=jnp.int32)[:, None, None]
    dense = jnp.sum(jnp.where(hit, shares[None], 0.0), axis=1)
    both = jnp.stack([dense, swap(dense)])
    routes = jnp.stack([both] + [along(both, m) for m in range(1, stages)])
    routes = routes.reshape(stages, 2, groups, length, tokens)
    routes = lax.dynamic_index_in_dim(routes, place, axis=3, keepdims=False)
    routes = jnp.stack(
        [
            lax.dynamic_index_in_dim(routes, group ^ k, axis=2, keepdims=False)
            for k in range(groups)
        ],
        axis=2,
    ).reshape(stages * 2 * groups, tokens)

    inside = call(inside_kernel, [((tokens, inner), F32)])(queries, keys, values)[0]
    ranks = call(rank_kernel, [(routes.shape, F32)])(routes)[0]
    total = arrived[0].astype(F32)
    for more in arrived[1:]:
        total = total + more.astype(F32)
    mine = total.astype(BF)
    other = swap(mine)
    residual, moe_in = call(
        project_kernel, [((tokens, features), BF)] * 2, [pltpu.VMEM((tokens, inner), BF)]
    )(
        core.reshape(1),
        inside,
        queries,
        mine,
        other,
        pair,
        lin_gain.reshape(1, inner),
        resid_in.reshape(tokens, features),
        out_proj,
        moe_gain.reshape(1, features),
    )

    routing = sending(stages)
    returning = homing(stages)
    blocks = {0: moe_in}
    outs = {}
    partners = {0: swap(moe_in)}
    for m in range(1, stages):
        source, shift = routing[m]
        blocks[m] = along(blocks[source], shift)
    for m in range(stages):
        base = m * 2 * groups
        partner = swap(blocks[m]) if m else partners[0]
        picked = select(slots, groups, base, blocks[m], partner, ranks)
        taken = [across(picked[k], k) for k in range(groups)]
        outs[m] = experts(taken, gate_weight, up_weight, down_weight)
    sums = {m: [] for m in range(stages)}
    for m in back_order(stages):
        base = m * 2 * groups
        backs = [across(outs[m][k], k) for k in range(groups)]
        own, par = combine(slots, base, backs, ranks, routes)
        part = own.astype(F32) + swap(par).astype(F32)
        for more in sums[m]:
            part = part + more.astype(F32)
        if m:
            into, shift = returning[m]
            sums[into].append(along(part.astype(BF), shift))
    combined = residual.astype(F32) + part
    return combined.astype(BF).reshape(1, tokens, features)


def sending(stages):
    if stages == 4:
        return {1: (0, 1), 2: (0, 2), 3: (2, 1)}
    return {m: (0, m) for m in range(1, stages)}


def homing(stages):
    if stages == 4:
        return {2: (3, 1), 3: (0, 3), 1: (0, 1)}
    return {m: (0, m) for m in range(1, stages)}


def back_order(stages):
    return list(range(2, stages)) + [1, 0]


def solution(mesh):
    rows = P("grp", "seq", None)
    held = P(("grp", "seq"), None, None)
    in_specs = (rows, rows, rows, rows, P(), P(), P(), rows, rows, held, held, held)

    return jax.shard_map(on_device, mesh=mesh, in_specs=in_specs, out_specs=rows, check_vma=False)
```

```python
import functools

import jax
import jax.numpy as jnp
from jax import lax
from jax.experimental import pallas as pl
from jax.experimental.pallas import tpu as pltpu
from jax.sharding import PartitionSpec as P


HEAD = 128
TOP = 8
epsilon = 1e-06
BF = jnp.bfloat16
F32 = jnp.float32


def dot(a, b, ca=1, cb=0):
    return lax.dot_general(a, b, (((ca,), (cb,)), ((), ())), preferred_element_type=F32)


def call(body, outs, scratch=(), limit=24, away=()):
    def run(*args):
        specs = []
        placed = []
        for i, x in enumerate(args):
            space = pltpu.SMEM if x.size == 1 else pltpu.VMEM
            if i in away:
                space = pltpu.HBM
            specs.append(pl.BlockSpec(memory_space=space))
            placed.append(pltpu.with_memory_space_constraint(x, space))
        return pl.pallas_call(
            body,
            in_specs=specs,
            out_specs=[pl.BlockSpec(memory_space=pltpu.VMEM)] * len(outs),
            out_shape=[pltpu.VMEM(shape, dtype) for shape, dtype in outs],
            scratch_shapes=list(scratch),
            compiler_params=pltpu.CompilerParams(vmem_limit_bytes=limit << 20),
        )(*placed)

    return run


def column_copies(pairs, sems):
    parts = sems.shape[1]
    copies = []
    for i in range(parts):
        for n, (src, dst) in enumerate(pairs):
            width = dst.shape[1] // parts
            cols = pl.ds(i * width, width)
            copy = pltpu.make_async_copy(src.at[:, cols], dst.at[:, cols], sems.at[n, i])
            copy.start()
            copies.append(copy)

    def wait(i):
        for copy in copies[i * len(pairs) : (i + 1) * len(pairs)]:
            copy.wait()

    return wait


def state_kernel(k_hbm, v_hbm, s_ref, k_ref, v_ref, sems):
    heads = k_ref.shape[1] // HEAD
    parts = sems.shape[1]
    wait = column_copies([(k_hbm, k_ref), (v_hbm, v_ref)], sems)
    for i in range(parts):
        wait(i)
        for h in range(i * heads // parts, (i + 1) * heads // parts):
            cols = slice(h * HEAD, (h + 1) * HEAD)
            s_ref[cols, :] = dot(k_ref[:, cols], v_ref[:, cols], 0, 0).astype(BF)


def inside_kernel(
    q_hbm, k_hbm, v_hbm, w_hbm, core_ref, group_ref, place_ref,
    o_ref, w_ref, q_ref, k_ref, v_ref, sems, w_sem,
):
    tokens = q_ref.shape[0]
    heads = q_ref.shape[1] // HEAD
    parts = sems.shape[1]
    wait = column_copies([(q_hbm, q_ref), (k_hbm, k_ref), (v_hbm, v_ref)], sems)
    bring = pltpu.make_async_copy(w_hbm, w_ref, w_sem)
    bring.start()
    rows = lax.broadcasted_iota(jnp.int32, (tokens, tokens), 0)
    cols = lax.broadcasted_iota(jnp.int32, (tokens, tokens), 1)
    causal = rows >= cols
    for h in range(heads):
        if h % (heads // parts) == 0:
            wait(h // (heads // parts))
        part = slice(h * HEAD, (h + 1) * HEAD)
        scores = dot(q_ref[:, part], k_ref[:, part], 1, 1)
        scores = jnp.where(causal, scores, 0.0).astype(BF)
        o_ref[:, part] = dot(scores, v_ref[:, part])
    bring.wait()


def add_kernel(*refs):
    total = refs[0][...].astype(F32)
    for more in refs[1:-1]:
        total = total + more[...].astype(F32)
    refs[-1][...] = total.astype(BF)


def added(*parts):
    return call(add_kernel, [(parts[0].shape, BF)])(*parts)[0]


def project_kernel(
    core_ref, in_ref, q_ref, mine_ref, other_ref, pair_ref, gain_ref, resid_ref, w_ref, mgain_ref,
    res_ref, moe_ref, normed_ref,
):
    core = core_ref[0]
    heads = q_ref.shape[1] // HEAD
    half = heads // 2
    low = core == 0
    second = jnp.where(low, 0.0, 1.0)
    for h in range(heads):
        part = slice(h * HEAD, (h + 1) * HEAD)
        at = slice((h % half) * HEAD, (h % half + 1) * HEAD)
        first = low if h < half else jnp.logical_not(low)
        prefix = jnp.where(first, mine_ref[at, :].astype(F32), other_ref[at, :].astype(F32))
        carried = (prefix + second * pair_ref[part, :].astype(F32)).astype(BF)
        attended = in_ref[:, part] + dot(q_ref[:, part], carried)
        mean = jnp.mean(attended * attended, axis=1, keepdims=True)
        normed_ref[:, part] = (attended * lax.rsqrt(mean + epsilon) * gain_ref[:, part]).astype(BF)
    features = res_ref.shape[1]
    width = features // 4
    square = jnp.zeros((res_ref.shape[0], 1), F32)
    for i in range(4):
        at = slice(i * width, (i + 1) * width)
        added = resid_ref[:, at].astype(F32) + dot(normed_ref[...], w_ref[:, at])
        rounded = added.astype(BF)
        res_ref[:, at] = rounded
        wide = rounded.astype(F32)
        square = square + jnp.sum(wide * wide, axis=1, keepdims=True)
    scale = lax.rsqrt(square / features + epsilon)
    moe_ref[...] = (res_ref[...].astype(F32) * scale * mgain_ref[...]).astype(BF)


def pack_kernel(own_ref, par_ref, out_ref):
    count = own_ref.shape[0]
    out_ref[:count, :] = own_ref[...]
    out_ref[count:, :] = par_ref[...]


def rank_kernel(groups, length, group_ref, place_ref, *refs):
    packs = refs[:-2]
    route_ref, rank_ref = refs[-2:]
    count = groups * length
    place = place_ref[0]
    group = group_ref[0]
    row = 0
    for pack in packs:
        for block in range(2):
            for k in range(groups):
                at = block * count + (group ^ k) * length + place
                route_ref[row : row + 1, :] = pack[pl.ds(at, 1), :]
                row += 1
    tokens = route_ref.shape[1]
    rows = lax.broadcasted_iota(jnp.int32, (tokens, tokens), 0)
    cols = lax.broadcasted_iota(jnp.int32, (tokens, tokens), 1)
    earlier = jnp.where(rows < cols, 1.0, 0.0).astype(BF)
    named = route_ref[...] > 0.0
    rank = dot(jnp.where(named, 1.0, 0.0).astype(BF), earlier)
    rank_ref[...] = jnp.where(named, rank, -1.0)


def slots_of(rank_ref, value, row, slots):
    rank = rank_ref[row : row + 1, :]
    number = lax.broadcasted_iota(jnp.int32, (slots, rank.shape[1]), 0).astype(F32)
    return jnp.where(number == rank, value, 0.0)


def select_kernel(slots, base, own_ref, par_ref, rank_ref, *outs):
    groups = len(outs)
    picks = []
    for block in range(2):
        rows = [slots_of(rank_ref, 1.0, base + block * groups + k, slots) for k in range(groups)]
        picks.append(jnp.concatenate(rows, axis=0).astype(BF))
    first = dot(picks[0], own_ref[...])
    second = dot(picks[1], par_ref[...])
    for k in range(groups):
        at = slice(k * slots, (k + 1) * slots)
        outs[k][...] = jnp.concatenate([first[at], second[at]], axis=0).astype(BF)


def select(slots, groups, base, own, par, rank):
    shape = ((2 * slots, own.shape[1]), BF)
    body = functools.partial(select_kernel, slots, base)
    return call(body, [shape] * groups)(own, par, rank)


def combine_kernel(slots, groups, base, *refs):
    backs = refs[:groups]
    rank_ref, weight_ref, own_ref, par_ref = refs[groups:]
    rows = jnp.concatenate([r[...] for r in backs], axis=0)
    zero = jnp.zeros((slots, rank_ref.shape[1]), F32)
    sides = []
    for block in range(2):
        parts = []
        for k in range(groups):
            row = base + block * groups + k
            mine = slots_of(rank_ref, weight_ref[row : row + 1, :], row, slots)
            parts += [mine, zero] if block == 0 else [zero, mine]
        sides.append(jnp.concatenate(parts, axis=0).astype(BF))
    own_ref[...] = dot(sides[0], rows, 0, 0).astype(BF)
    par_ref[...] = dot(sides[1], rows, 0, 0).astype(BF)


def combine(slots, base, backs, rank, weight):
    shape = ((rank.shape[1], backs[0].shape[1]), BF)
    body = functools.partial(combine_kernel, slots, len(backs), base)
    return call(body, [shape] * 2)(*backs, rank, weight)


def expert_kernel(groups, *refs):
    xs = refs[:groups]
    gate_ref, up_ref, down_ref = refs[groups : groups + 3]
    outs = refs[groups + 3 : 2 * groups + 3]
    hidden_ref = refs[2 * groups + 3]
    rows, features = xs[0].shape
    units = gate_ref.shape[2]
    x = jnp.concatenate([r[...] for r in xs], axis=0)
    width = 256
    for j in range(units // width):
        at = slice(j * width, (j + 1) * width)
        gate = dot(x, gate_ref[0, :, at])
        up = dot(x, up_ref[0, :, at])
        hidden_ref[:, at] = (gate / (1.0 + jnp.exp(-gate)) * up).astype(BF)
    hidden = hidden_ref[...]
    width = 512
    for j in range(features // width):
        at = slice(j * width, (j + 1) * width)
        out = dot(hidden, down_ref[0, :, at]).astype(BF)
        for k in range(groups):
            outs[k][:, at] = out[k * rows : (k + 1) * rows]


def experts(xs, gate, up, down):
    groups = len(xs)
    body = functools.partial(expert_kernel, groups)
    scratch = [pltpu.VMEM((groups * xs[0].shape[0], gate.shape[2]), BF)]
    outs = [(xs[0].shape, BF)] * groups
    return call(body, outs, scratch)(*xs, gate, up, down)


def on_device(
    resid_in,
    lin_query,
    lin_key,
    lin_value,
    lin_gain,
    out_proj,
    moe_gain,
    expert_ids,
    route_scores,
    gate_weight,
    up_weight,
    down_weight,
):
    tokens = resid_in.shape[1]
    features = resid_in.shape[2]
    groups = lax.axis_size("grp")
    length = lax.axis_size("seq")
    stages = length // 2
    group = lax.axis_index("grp")
    place = lax.axis_index("seq")
    core = place % 2
    expert_count = gate_weight.shape[0] * groups * length
    capacity = tokens * TOP * 5 // (4 * expert_count)
    slots = -(-capacity // 8) * 8

    scalars = [x.reshape(1) for x in (core, group, place)]

    def swap(x):
        return lax.ppermute(x, "seq", [(s, s ^ 1) for s in range(length)])

    def along(x, m):
        return lax.ppermute(x, "seq", [(s, s ^ (2 * m)) for s in range(length)])

    def across(x, m):
        if m == 0:
            return x
        return lax.ppermute(x, "grp", [(g, g ^ m) for g in range(groups)])

    def later(x, m, froms):
        pairs = [(2 * z + c, 2 * (z + m) + c) for z in froms for c in range(2)]
        return lax.ppermute(x, "seq", pairs)

    queries = lin_query.reshape(tokens, -1)
    keys = lin_key.reshape(tokens, -1)
    values = lin_value.reshape(tokens, -1)
    inner = queries.shape[1]
    half = inner // 2

    states = call(
        state_kernel,
        [((inner, HEAD), BF)],
        [pltpu.VMEM(keys.shape, BF)] * 2 + [pltpu.SemaphoreType.DMA((2, 4))],
        away=(0, 1),
    )(keys, values)[0]
    pair = swap(states)
    summed = (states.astype(F32) + pair.astype(F32)).astype(BF)
    summed = lax.dynamic_slice_in_dim(summed, core * half, half, axis=0)
    if stages == 4:
        arrived = [later(summed, 1, range(3)), later(summed, 2, [0])]
        upto = added(summed, arrived[0])
        arrived.append(later(upto, 2, [1]))
    else:
        arrived = [later(summed, m, range(stages - m)) for m in range(1, stages)]

    chosen = expert_ids.reshape(tokens, TOP).T
    scores = route_scores.reshape(tokens, TOP)
    shares = (scores / jnp.sum(scores, axis=1, keepdims=True)).T
    hit = chosen[None] == jnp.arange(expert_count, dtype=jnp.int32)[:, None, None]
    dense = jnp.sum(jnp.where(hit, shares[None], 0.0), axis=1)
    shape = (2 * expert_count, tokens)
    both = call(pack_kernel, [(shape, F32)])(dense, swap(dense))[0]
    packs = [both] + [along(both, m) for m in range(1, stages)]

    inside, out_proj = call(
        inside_kernel,
        [((tokens, inner), F32), (out_proj.shape, BF)],
        [pltpu.VMEM(keys.shape, BF)] * 3
        + [pltpu.SemaphoreType.DMA((3, 4)), pltpu.SemaphoreType.DMA],
        away=(0, 1, 2, 3),
    )(queries, keys, values, out_proj, *scalars)
    shape = (stages * 2 * groups, tokens)
    body = functools.partial(rank_kernel, groups, length)
    routes, ranks = call(body, [(shape, F32)] * 2)(
        *scalars[1:], *packs
    )
    mine = added(*arrived)
    other = swap(mine)
    residual, moe_in = call(
        project_kernel, [((tokens, features), BF)] * 2, [pltpu.VMEM((tokens, inner), BF)]
    )(
        scalars[0],
        inside,
        queries,
        mine,
        other,
        pair,
        lin_gain.reshape(1, inner),
        resid_in.reshape(tokens, features),
        out_proj,
        moe_gain.reshape(1, features),
    )

    routing = sending(stages)
    returning = homing(stages)
    blocks = {0: moe_in}
    outs = {}
    partners = {0: swap(moe_in)}
    for m in range(1, stages):
        source, shift = routing[m]
        blocks[m] = along(blocks[source], shift)
    for m in range(stages):
        base = m * 2 * groups
        partner = swap(blocks[m]) if m else partners[0]
        picked = select(slots, groups, base, blocks[m], partner, ranks)
        taken = [across(picked[k], k) for k in range(groups)]
        outs[m] = experts(taken, gate_weight, up_weight, down_weight)
    sums = {m: [] for m in range(stages)}
    for m in back_order(stages):
        base = m * 2 * groups
        backs = [across(outs[m][k], k) for k in range(groups)]
        own, par = combine(slots, base, backs, ranks, routes)
        part = own.astype(F32) + swap(par).astype(F32)
        for more in sums[m]:
            part = part + more.astype(F32)
        if m:
            into, shift = returning[m]
            sums[into].append(along(part.astype(BF), shift))
    combined = residual.astype(F32) + part
    return combined.astype(BF).reshape(1, tokens, features)


def sending(stages):
    if stages == 4:
        return {1: (0, 1), 2: (0, 2), 3: (2, 1)}
    return {m: (0, m) for m in range(1, stages)}


def homing(stages):
    if stages == 4:
        return {2: (3, 1), 3: (0, 3), 1: (0, 1)}
    return {m: (0, m) for m in range(1, stages)}


def back_order(stages):
    return list(range(2, stages)) + [1, 0]


def solution(mesh):
    rows = P("grp", "seq", None)
    held = P(("grp", "seq"), None, None)
    in_specs = (rows, rows, rows, rows, P(), P(), P(), rows, rows, held, held, held)

    return jax.shard_map(on_device, mesh=mesh, in_specs=in_specs, out_specs=rows, check_vma=False)
```

```python
import functools

import jax
import jax.numpy as jnp
from jax import lax
from jax.experimental import pallas as pl
from jax.experimental.pallas import tpu as pltpu
from jax.sharding import PartitionSpec as P


HEAD = 128
TOP = 8
epsilon = 1e-06
BF = jnp.bfloat16
F32 = jnp.float32


def dot(a, b, ca=1, cb=0):
    return lax.dot_general(a, b, (((ca,), (cb,)), ((), ())), preferred_element_type=F32)


def call(body, outs, scratch=(), limit=24, away=()):
    def run(*args):
        specs = []
        placed = []
        for i, x in enumerate(args):
            space = pltpu.SMEM if x.size == 1 else pltpu.VMEM
            if i in away:
                space = pltpu.HBM
            specs.append(pl.BlockSpec(memory_space=space))
            placed.append(pltpu.with_memory_space_constraint(x, space))
        return pl.pallas_call(
            body,
            in_specs=specs,
            out_specs=[pl.BlockSpec(memory_space=pltpu.VMEM)] * len(outs),
            out_shape=[pltpu.VMEM(shape, dtype) for shape, dtype in outs],
            scratch_shapes=list(scratch),
            compiler_params=pltpu.CompilerParams(vmem_limit_bytes=limit << 20),
        )(*placed)

    return run


def column_copies(pairs, sems):
    parts = sems.shape[1]
    copies = []
    for i in range(parts):
        for n, (src, dst) in enumerate(pairs):
            width = dst.shape[1] // parts
            cols = pl.ds(i * width, width)
            copy = pltpu.make_async_copy(src.at[:, cols], dst.at[:, cols], sems.at[n, i])
            copy.start()
            copies.append(copy)

    def wait(i):
        for copy in copies[i * len(pairs) : (i + 1) * len(pairs)]:
            copy.wait()

    return wait


def state_kernel(k_hbm, v_hbm, s_ref, k_ref, v_ref, sems):
    heads = k_ref.shape[1] // HEAD
    parts = sems.shape[1]
    wait = column_copies([(k_hbm, k_ref), (v_hbm, v_ref)], sems)
    for i in range(parts):
        wait(i)
        for h in range(i * heads // parts, (i + 1) * heads // parts):
            cols = slice(h * HEAD, (h + 1) * HEAD)
            s_ref[cols, :] = dot(k_ref[:, cols], v_ref[:, cols], 0, 0).astype(BF)


def inside_kernel(
    q_hbm, k_hbm, v_hbm, w_hbm, core_ref, group_ref, place_ref,
    o_ref, w_ref, q_ref, k_ref, v_ref, sems, w_sem,
):
    tokens = q_ref.shape[0]
    heads = q_ref.shape[1] // HEAD
    parts = sems.shape[1]
    wait = column_copies([(q_hbm, q_ref), (k_hbm, k_ref), (v_hbm, v_ref)], sems)
    bring = pltpu.make_async_copy(w_hbm, w_ref, w_sem)
    bring.start()
    rows = lax.broadcasted_iota(jnp.int32, (tokens, tokens), 0)
    cols = lax.broadcasted_iota(jnp.int32, (tokens, tokens), 1)
    causal = rows >= cols
    for h in range(heads):
        if h % (heads // parts) == 0:
            wait(h // (heads // parts))
        part = slice(h * HEAD, (h + 1) * HEAD)
        scores = dot(q_ref[:, part], k_ref[:, part], 1, 1)
        scores = jnp.where(causal, scores, 0.0).astype(BF)
        o_ref[:, part] = dot(scores, v_ref[:, part])
    bring.wait()


def add_kernel(*refs):
    total = refs[0][...].astype(F32)
    for more in refs[1:-1]:
        total = total + more[...].astype(F32)
    refs[-1][...] = total.astype(BF)


def prefix_kernel(takes, place_ref, *refs):
    chip = lax.shift_right_logical(place_ref[0], 1)
    total = jnp.zeros(refs[-1].shape, F32)
    for chips, ref in zip(takes, refs):
        takes_it = functools.reduce(jnp.logical_or, [chip == z for z in chips])
        total = total + jnp.where(takes_it, ref[...].astype(F32), 0.0)
    refs[-1][...] = total.astype(BF)


def added(*parts):
    return call(add_kernel, [(parts[0].shape, BF)])(*parts)[0]


def project_kernel(
    core_ref, in_ref, q_ref, mine_ref, other_ref, pair_ref, gain_ref, resid_ref, w_ref, mgain_ref,
    res_ref, moe_ref, normed_ref,
):
    core = core_ref[0]
    heads = q_ref.shape[1] // HEAD
    half = heads // 2
    low = core == 0
    second = jnp.where(low, 0.0, 1.0)
    for h in range(heads):
        part = slice(h * HEAD, (h + 1) * HEAD)
        at = slice((h % half) * HEAD, (h % half + 1) * HEAD)
        first = low if h < half else jnp.logical_not(low)
        prefix = jnp.where(first, mine_ref[at, :].astype(F32), other_ref[at, :].astype(F32))
        carried = (prefix + second * pair_ref[part, :].astype(F32)).astype(BF)
        attended = in_ref[:, part] + dot(q_ref[:, part], carried)
        mean = jnp.mean(attended * attended, axis=1, keepdims=True)
        normed_ref[:, part] = (attended * lax.rsqrt(mean + epsilon) * gain_ref[:, part]).astype(BF)
    features = res_ref.shape[1]
    width = features // 4
    square = jnp.zeros((res_ref.shape[0], 1), F32)
    for i in range(4):
        at = slice(i * width, (i + 1) * width)
        added = resid_ref[:, at].astype(F32) + dot(normed_ref[...], w_ref[:, at])
        rounded = added.astype(BF)
        res_ref[:, at] = rounded
        wide = rounded.astype(F32)
        square = square + jnp.sum(wide * wide, axis=1, keepdims=True)
    scale = lax.rsqrt(square / features + epsilon)
    moe_ref[...] = (res_ref[...].astype(F32) * scale * mgain_ref[...]).astype(BF)


def pack_kernel(own_ref, par_ref, out_ref):
    count = own_ref.shape[0]
    out_ref[:count, :] = own_ref[...]
    out_ref[count:, :] = par_ref[...]


def rank_kernel(groups, length, group_ref, place_ref, *refs):
    packs = refs[:-2]
    route_ref, rank_ref = refs[-2:]
    count = groups * length
    place = place_ref[0]
    group = group_ref[0]
    row = 0
    for pack in packs:
        for block in range(2):
            for k in range(groups):
                at = block * count + (group ^ k) * length + place
                route_ref[row : row + 1, :] = pack[pl.ds(at, 1), :]
                row += 1
    tokens = route_ref.shape[1]
    rows = lax.broadcasted_iota(jnp.int32, (tokens, tokens), 0)
    cols = lax.broadcasted_iota(jnp.int32, (tokens, tokens), 1)
    earlier = jnp.where(rows < cols, 1.0, 0.0).astype(BF)
    named = route_ref[...] > 0.0
    rank = dot(jnp.where(named, 1.0, 0.0).astype(BF), earlier)
    rank_ref[...] = jnp.where(named, rank, -1.0)


def slots_of(rank_ref, value, row, slots):
    rank = rank_ref[row : row + 1, :]
    number = lax.broadcasted_iota(jnp.int32, (slots, rank.shape[1]), 0).astype(F32)
    return jnp.where(number == rank, value, 0.0)


def select_kernel(slots, base, own_ref, par_ref, rank_ref, *outs):
    groups = len(outs)
    picks = []
    for block in range(2):
        rows = [slots_of(rank_ref, 1.0, base + block * groups + k, slots) for k in range(groups)]
        picks.append(jnp.concatenate(rows, axis=0).astype(BF))
    first = dot(picks[0], own_ref[...])
    second = dot(picks[1], par_ref[...])
    for k in range(groups):
        at = slice(k * slots, (k + 1) * slots)
        outs[k][...] = jnp.concatenate([first[at], second[at]], axis=0).astype(BF)


def select(slots, groups, base, own, par, rank):
    shape = ((2 * slots, own.shape[1]), BF)
    body = functools.partial(select_kernel, slots, base)
    return call(body, [shape] * groups)(own, par, rank)


def combine_kernel(slots, groups, base, *refs):
    backs = refs[:groups]
    rank_ref, weight_ref, own_ref, par_ref = refs[groups:]
    rows = jnp.concatenate([r[...] for r in backs], axis=0)
    zero = jnp.zeros((slots, rank_ref.shape[1]), F32)
    sides = []
    for block in range(2):
        parts = []
        for k in range(groups):
            row = base + block * groups + k
            mine = slots_of(rank_ref, weight_ref[row : row + 1, :], row, slots)
            parts += [mine, zero] if block == 0 else [zero, mine]
        sides.append(jnp.concatenate(parts, axis=0).astype(BF))
    own_ref[...] = dot(sides[0], rows, 0, 0).astype(BF)
    par_ref[...] = dot(sides[1], rows, 0, 0).astype(BF)


def combine(slots, base, backs, rank, weight):
    shape = ((rank.shape[1], backs[0].shape[1]), BF)
    body = functools.partial(combine_kernel, slots, len(backs), base)
    return call(body, [shape] * 2)(*backs, rank, weight)


def expert_kernel(groups, *refs):
    xs = refs[:groups]
    gate_ref, up_ref, down_ref = refs[groups : groups + 3]
    outs = refs[groups + 3 : 2 * groups + 3]
    hidden_ref = refs[2 * groups + 3]
    rows, features = xs[0].shape
    units = gate_ref.shape[2]
    x = jnp.concatenate([r[...] for r in xs], axis=0)
    width = 256
    for j in range(units // width):
        at = slice(j * width, (j + 1) * width)
        gate = dot(x, gate_ref[0, :, at])
        up = dot(x, up_ref[0, :, at])
        hidden_ref[:, at] = (gate / (1.0 + jnp.exp(-gate)) * up).astype(BF)
    hidden = hidden_ref[...]
    width = 512
    for j in range(features // width):
        at = slice(j * width, (j + 1) * width)
        out = dot(hidden, down_ref[0, :, at]).astype(BF)
        for k in range(groups):
            outs[k][:, at] = out[k * rows : (k + 1) * rows]


def experts(xs, gate, up, down):
    groups = len(xs)
    body = functools.partial(expert_kernel, groups)
    scratch = [pltpu.VMEM((groups * xs[0].shape[0], gate.shape[2]), BF)]
    outs = [(xs[0].shape, BF)] * groups
    return call(body, outs, scratch)(*xs, gate, up, down)


def on_device(
    resid_in,
    lin_query,
    lin_key,
    lin_value,
    lin_gain,
    out_proj,
    moe_gain,
    expert_ids,
    route_scores,
    gate_weight,
    up_weight,
    down_weight,
):
    tokens = resid_in.shape[1]
    features = resid_in.shape[2]
    groups = lax.axis_size("grp")
    length = lax.axis_size("seq")
    stages = length // 2
    group = lax.axis_index("grp")
    place = lax.axis_index("seq")
    core = place % 2
    expert_count = gate_weight.shape[0] * groups * length
    capacity = tokens * TOP * 5 // (4 * expert_count)
    slots = -(-capacity // 8) * 8

    scalars = [x.reshape(1) for x in (core, group, place)]

    def swap(x):
        return lax.ppermute(x, "seq", [(s, s ^ 1) for s in range(length)])

    def along(x, m):
        return lax.ppermute(x, "seq", [(s, s ^ (2 * m)) for s in range(length)])

    def across(x, m):
        if m == 0:
            return x
        return lax.ppermute(x, "grp", [(g, g ^ m) for g in range(groups)])

    def between(x, chips):
        both = list(chips) + [(b, a) for a, b in chips]
        return lax.ppermute(
            x, "seq", sorted((2 * a + c, 2 * b + c) for a, b in both for c in range(2))
        )

    def onward(x, chips):
        return lax.ppermute(
            x, "seq", sorted((2 * a + c, 2 * b + c) for a, b in chips for c in range(2))
        )

    def later(x, m, froms):
        pairs = [(2 * z + c, 2 * (z + m) + c) for z in froms for c in range(2)]
        return lax.ppermute(x, "seq", pairs)

    queries = lin_query.reshape(tokens, -1)
    keys = lin_key.reshape(tokens, -1)
    values = lin_value.reshape(tokens, -1)
    inner = queries.shape[1]
    half = inner // 2

    states = call(
        state_kernel,
        [((inner, HEAD), BF)],
        [pltpu.VMEM(keys.shape, BF)] * 2 + [pltpu.SemaphoreType.DMA((2, 4))],
        away=(0, 1),
    )(keys, values)[0]
    pair = swap(states)
    summed = (states.astype(F32) + pair.astype(F32)).astype(BF)
    summed = lax.dynamic_slice_in_dim(summed, core * half, half, axis=0)
    if stages == 4:
        arrived = [
            between(summed, [(0, 1), (2, 3)]), between(summed, [(1, 2)]), between(summed, [(0, 2)])
        ]
        arrived.append(between(added(summed, arrived[0]), [(1, 3)]))
    else:
        arrived = [later(summed, m, range(stages - m)) for m in range(1, stages)]

    chosen = expert_ids.reshape(tokens, TOP).T
    scores = route_scores.reshape(tokens, TOP)
    shares = (scores / jnp.sum(scores, axis=1, keepdims=True)).T
    hit = chosen[None] == jnp.arange(expert_count, dtype=jnp.int32)[:, None, None]
    dense = jnp.sum(jnp.where(hit, shares[None], 0.0), axis=1)
    shape = (2 * expert_count, tokens)
    both = call(pack_kernel, [(shape, F32)])(dense, swap(dense))[0]
    packs = [both] + [along(both, m) for m in range(1, stages)]

    inside, out_proj = call(
        inside_kernel,
        [((tokens, inner), F32), (out_proj.shape, BF)],
        [pltpu.VMEM(keys.shape, BF)] * 3
        + [pltpu.SemaphoreType.DMA((3, 4)), pltpu.SemaphoreType.DMA],
        away=(0, 1, 2, 3),
    )(queries, keys, values, out_proj, *scalars)
    shape = (stages * 2 * groups, tokens)
    body = functools.partial(rank_kernel, groups, length)
    routes, ranks = call(body, [(shape, F32)] * 2)(
        *scalars[1:], *packs
    )
    if stages == 4:
        takes = [(1, 3), (2,), (2,), (3,)]
        body = functools.partial(prefix_kernel, takes)
        mine = call(body, [(summed.shape, BF)])(scalars[2], *arrived)[0]
    else:
        mine = added(*arrived)
    other = swap(mine)
    residual, moe_in = call(
        project_kernel, [((tokens, features), BF)] * 2, [pltpu.VMEM((tokens, inner), BF)]
    )(
        scalars[0],
        inside,
        queries,
        mine,
        other,
        pair,
        lin_gain.reshape(1, inner),
        resid_in.reshape(tokens, features),
        out_proj,
        moe_gain.reshape(1, features),
    )

    returning = homing(stages)
    blocks = {0: moe_in}
    outs = {}
    partners = {0: swap(moe_in)}
    if stages == 4:
        blocks[1] = between(moe_in, [(0, 1), (2, 3)])
        across_middle = between(moe_in, [(1, 2)])
        outward = [(1, 0), (2, 3)]
        near = onward(across_middle, outward)
        far = between(blocks[1], [(1, 2)])
        blocks[2] = added(near, far)
        blocks[3] = added(across_middle, onward(far, outward))
    else:
        for m in range(1, stages):
            blocks[m] = along(moe_in, m)
    for m in range(stages):
        base = m * 2 * groups
        partner = swap(blocks[m]) if m else partners[0]
        picked = select(slots, groups, base, blocks[m], partner, ranks)
        taken = [across(picked[k], k) for k in range(groups)]
        outs[m] = experts(taken, gate_weight, up_weight, down_weight)
    sums = {m: [] for m in range(stages)}
    for m in back_order(stages):
        base = m * 2 * groups
        backs = [across(outs[m][k], k) for k in range(groups)]
        own, par = combine(slots, base, backs, ranks, routes)
        part = own.astype(F32) + swap(par).astype(F32)
        for more in sums[m]:
            part = part + more.astype(F32)
        if m:
            into, shift = returning[m]
            sums[into].append(along(part.astype(BF), shift))
    combined = residual.astype(F32) + part
    return combined.astype(BF).reshape(1, tokens, features)


def homing(stages):
    if stages == 4:
        return {2: (3, 1), 3: (0, 3), 1: (0, 1)}
    return {m: (0, m) for m in range(1, stages)}


def back_order(stages):
    return list(range(2, stages)) + [1, 0]


def solution(mesh):
    rows = P("grp", "seq", None)
    held = P(("grp", "seq"), None, None)
    in_specs = (rows, rows, rows, rows, P(), P(), P(), rows, rows, held, held, held)

    return jax.shard_map(on_device, mesh=mesh, in_specs=in_specs, out_specs=rows, check_vma=False)
```

```python
import functools

import jax
import jax.numpy as jnp
from jax import lax
from jax.experimental import pallas as pl
from jax.experimental.pallas import tpu as pltpu
from jax.sharding import PartitionSpec as P


HEAD = 128
TOP = 8
epsilon = 1e-06
BF = jnp.bfloat16
F32 = jnp.float32


def dot(a, b, ca=1, cb=0):
    return lax.dot_general(a, b, (((ca,), (cb,)), ((), ())), preferred_element_type=F32)


def call(body, outs, scratch=(), limit=24, away=(), leave=False):
    def run(*args):
        specs = []
        placed = []
        for i, x in enumerate(args):
            space = pltpu.SMEM if x.size == 1 else pltpu.VMEM
            if i in away:
                space = pltpu.HBM
            specs.append(pl.BlockSpec(memory_space=space))
            placed.append(pltpu.with_memory_space_constraint(x, space))
        return pl.pallas_call(
            body,
            in_specs=specs,
            out_specs=[pl.BlockSpec(memory_space=pltpu.VMEM)] * len(outs),
            out_shape=[
                jax.ShapeDtypeStruct(shape, dtype) if leave else pltpu.VMEM(shape, dtype)
                for shape, dtype in outs
            ],
            scratch_shapes=list(scratch),
            compiler_params=pltpu.CompilerParams(vmem_limit_bytes=limit << 20),
        )(*placed)

    return run


def column_copies(pairs, sems):
    parts = sems.shape[1]
    copies = []
    for i in range(parts):
        for n, (src, dst) in enumerate(pairs):
            width = dst.shape[1] // parts
            cols = pl.ds(i * width, width)
            copy = pltpu.make_async_copy(src.at[:, cols], dst.at[:, cols], sems.at[n, i])
            copy.start()
            copies.append(copy)

    def wait(i):
        for copy in copies[i * len(pairs) : (i + 1) * len(pairs)]:
            copy.wait()

    return wait


def state_kernel(k_hbm, v_hbm, s_ref, k_ref, v_ref, sems):
    heads = k_ref.shape[1] // HEAD
    parts = sems.shape[1]
    wait = column_copies([(k_hbm, k_ref), (v_hbm, v_ref)], sems)
    for i in range(parts):
        wait(i)
        for h in range(i * heads // parts, (i + 1) * heads // parts):
            cols = slice(h * HEAD, (h + 1) * HEAD)
            s_ref[cols, :] = dot(k_ref[:, cols], v_ref[:, cols], 0, 0).astype(BF)


def inside_kernel(
    q_hbm, k_hbm, v_hbm, w_hbm, core_ref, group_ref, place_ref,
    o_ref, w_ref, q_ref, k_ref, v_ref, sems, w_sem,
):
    tokens = q_ref.shape[0]
    heads = q_ref.shape[1] // HEAD
    parts = sems.shape[1]
    wait = column_copies([(q_hbm, q_ref), (k_hbm, k_ref), (v_hbm, v_ref)], sems)
    bring = pltpu.make_async_copy(w_hbm, w_ref, w_sem)
    bring.start()
    rows = lax.broadcasted_iota(jnp.int32, (tokens, tokens), 0)
    cols = lax.broadcasted_iota(jnp.int32, (tokens, tokens), 1)
    causal = rows >= cols
    for h in range(heads):
        if h % (heads // parts) == 0:
            wait(h // (heads // parts))
        part = slice(h * HEAD, (h + 1) * HEAD)
        scores = dot(q_ref[:, part], k_ref[:, part], 1, 1)
        scores = jnp.where(causal, scores, 0.0).astype(BF)
        o_ref[:, part] = dot(scores, v_ref[:, part])
    bring.wait()


def add_kernel(*refs):
    total = refs[0][...].astype(F32)
    for more in refs[1:-1]:
        total = total + more[...].astype(F32)
    refs[-1][...] = total.astype(BF)


def added(*parts):
    return call(add_kernel, [(parts[0].shape, BF)])(*parts)[0]


def project_kernel(
    core_ref, in_ref, q_ref, mine_ref, other_ref, pair_ref, gain_ref, resid_ref, w_ref, mgain_ref,
    res_ref, moe_ref, normed_ref,
):
    core = core_ref[0]
    heads = q_ref.shape[1] // HEAD
    half = heads // 2
    low = core == 0
    second = jnp.where(low, 0.0, 1.0)
    for h in range(heads):
        part = slice(h * HEAD, (h + 1) * HEAD)
        at = slice((h % half) * HEAD, (h % half + 1) * HEAD)
        first = low if h < half else jnp.logical_not(low)
        prefix = jnp.where(first, mine_ref[at, :].astype(F32), other_ref[at, :].astype(F32))
        carried = (prefix + second * pair_ref[part, :].astype(F32)).astype(BF)
        attended = in_ref[:, part] + dot(q_ref[:, part], carried)
        mean = jnp.mean(attended * attended, axis=1, keepdims=True)
        normed_ref[:, part] = (attended * lax.rsqrt(mean + epsilon) * gain_ref[:, part]).astype(BF)
    features = res_ref.shape[1]
    width = features // 4
    square = jnp.zeros((res_ref.shape[0], 1), F32)
    for i in range(4):
        at = slice(i * width, (i + 1) * width)
        added = resid_ref[:, at].astype(F32) + dot(normed_ref[...], w_ref[:, at])
        rounded = added.astype(BF)
        res_ref[:, at] = rounded
        wide = rounded.astype(F32)
        square = square + jnp.sum(wide * wide, axis=1, keepdims=True)
    scale = lax.rsqrt(square / features + epsilon)
    moe_ref[...] = (res_ref[...].astype(F32) * scale * mgain_ref[...]).astype(BF)


def pack_kernel(own_ref, par_ref, out_ref):
    count = own_ref.shape[0]
    out_ref[:count, :] = own_ref[...]
    out_ref[count:, :] = par_ref[...]


def rank_kernel(groups, length, group_ref, place_ref, *refs):
    packs = refs[:-2]
    route_ref, rank_ref = refs[-2:]
    count = groups * length
    place = place_ref[0]
    group = group_ref[0]
    row = 0
    for straight in range(2):
        for pack in packs:
            for side in range(2):
                for k in range(groups):
                    at = (group ^ k) * length
                    at = at + ((place ^ side) if straight else side * count + place)
                    route_ref[row : row + 1, :] = pack[pl.ds(at, 1), :]
                    row += 1
    tokens = route_ref.shape[1]
    rows = lax.broadcasted_iota(jnp.int32, (tokens, tokens), 0)
    cols = lax.broadcasted_iota(jnp.int32, (tokens, tokens), 1)
    earlier = jnp.where(rows < cols, 1.0, 0.0).astype(BF)
    named = route_ref[...] > 0.0
    rank = dot(jnp.where(named, 1.0, 0.0).astype(BF), earlier)
    rank_ref[...] = jnp.where(named, rank, -1.0)


def slots_of(rank_ref, value, row, slots):
    rank = rank_ref[row : row + 1, :]
    number = lax.broadcasted_iota(jnp.int32, (slots, rank.shape[1]), 0).astype(F32)
    return jnp.where(number == rank, value, 0.0)


def select_kernel(slots, base, own_ref, par_ref, rank_ref, *outs):
    groups = len(outs)
    picks = []
    for block in range(2):
        rows = [slots_of(rank_ref, 1.0, base + block * groups + k, slots) for k in range(groups)]
        picks.append(jnp.concatenate(rows, axis=0).astype(BF))
    first = dot(picks[0], own_ref[...])
    second = dot(picks[1], par_ref[...])
    for k in range(groups):
        at = slice(k * slots, (k + 1) * slots)
        outs[k][...] = jnp.concatenate([first[at], second[at]], axis=0).astype(BF)


def select(slots, groups, base, own, par, rank):
    shape = ((2 * slots, own.shape[1]), BF)
    body = functools.partial(select_kernel, slots, base)
    return call(body, [shape] * groups)(own, par, rank)


def combine_kernel(slots, groups, base, *refs):
    backs = refs[:groups]
    rank_ref, weight_ref, own_ref, par_ref = refs[groups:]
    rows = jnp.concatenate([r[...] for r in backs], axis=0)
    zero = jnp.zeros((slots, rank_ref.shape[1]), F32)
    sides = []
    for block in range(2):
        parts = []
        for k in range(groups):
            row = base + block * groups + k
            mine = slots_of(rank_ref, weight_ref[row : row + 1, :], row, slots)
            parts += [mine, zero] if block == 0 else [zero, mine]
        sides.append(jnp.concatenate(parts, axis=0).astype(BF))
    own_ref[...] = dot(sides[0], rows, 0, 0).astype(BF)
    par_ref[...] = dot(sides[1], rows, 0, 0).astype(BF)


def combine(slots, base, backs, rank, weight):
    shape = ((rank.shape[1], backs[0].shape[1]), BF)
    body = functools.partial(combine_kernel, slots, len(backs), base)
    return call(body, [shape] * 2)(*backs, rank, weight)


def straight_select_kernel(slots, base, own_ref, rank_ref, *outs):
    rows = [slots_of(rank_ref, 1.0, base + i, slots) for i in range(len(outs))]
    picked = dot(jnp.concatenate(rows, axis=0).astype(BF), own_ref[...]).astype(BF)
    for i, out in enumerate(outs):
        out[...] = picked[i * slots : (i + 1) * slots]


def straight_select(slots, count, base, own, rank):
    body = functools.partial(straight_select_kernel, slots, base)
    shape = ((slots, own.shape[1]), BF)
    return call(body, [shape] * count)(own, rank)


def straight_combine_kernel(slots, count, base, *refs):
    backs = refs[:count]
    rank_ref, weight_ref = refs[count : count + 2]
    more = refs[count + 2 : -1]
    rows = stacked(backs)
    parts = []
    for i in range(count):
        row = base + i
        parts.append(slots_of(rank_ref, weight_ref[row : row + 1, :], row, slots))
    total = dot(jnp.concatenate(parts, axis=0).astype(BF), rows, 0, 0)
    for ref in more:
        total = total + ref[...].astype(F32)
    refs[-1][...] = total.astype(BF)


def straight_combine(slots, base, backs, rank, weight, more, leave):
    body = functools.partial(straight_combine_kernel, slots, len(backs), base)
    shape = ((rank.shape[1], backs[0].shape[1]), BF)
    return call(body, [shape], leave=leave)(*backs, rank, weight, *more)[0]


def stacked(refs):
    if refs[0].shape[0] % 16 == 0:
        return jnp.concatenate([r[...] for r in refs], axis=0)
    return jnp.concatenate([r[...].astype(F32) for r in refs], axis=0).astype(BF)


def expert_kernel(count, starts, *refs):
    xs = refs[:count]
    gate_ref, up_ref, down_ref = refs[count : count + 3]
    outs = refs[count + 3 : -1]
    hidden_ref = refs[-1]
    features = xs[0].shape[1]
    units = gate_ref.shape[2]
    x = stacked(xs)
    width = 256
    for j in range(units // width):
        at = slice(j * width, (j + 1) * width)
        gate = dot(x, gate_ref[0, :, at])
        up = dot(x, up_ref[0, :, at])
        hidden_ref[:, at] = (gate / (1.0 + jnp.exp(-gate)) * up).astype(BF)
    hidden = hidden_ref[...]
    width = 512
    for j in range(features // width):
        at = slice(j * width, (j + 1) * width)
        out = dot(hidden, down_ref[0, :, at])
        for ref, start in zip(outs, starts):
            ref[:, at] = out[start : start + ref.shape[0]].astype(BF)


def experts(xs, straight_in, straight_out, groups, gate, up, down):
    total = sum(x.shape[0] for x in xs)
    features = xs[0].shape[1]
    slots = total // (2 * groups)
    if straight_out:
        count, rows = 2 * groups, slots
        starts = [
            (side * groups + k if straight_in else 2 * k + side) * slots
            for side in range(2)
            for k in range(groups)
        ]
    else:
        count, rows = groups, 2 * slots
        starts = [k * rows for k in range(groups)]
    body = functools.partial(expert_kernel, len(xs), starts)
    scratch = [pltpu.VMEM((total, gate.shape[2]), BF)]
    return call(body, [((rows, features), BF)] * count, scratch)(*xs, gate, up, down)


def on_device(
    resid_in,
    lin_query,
    lin_key,
    lin_value,
    lin_gain,
    out_proj,
    moe_gain,
    expert_ids,
    route_scores,
    gate_weight,
    up_weight,
    down_weight,
):
    tokens = resid_in.shape[1]
    features = resid_in.shape[2]
    groups = lax.axis_size("grp")
    length = lax.axis_size("seq")
    stages = length // 2
    group = lax.axis_index("grp")
    place = lax.axis_index("seq")
    core = place % 2
    expert_count = gate_weight.shape[0] * groups * length
    capacity = tokens * TOP * 5 // (4 * expert_count)
    slots = -(-capacity // 8) * 8

    scalars = [x.reshape(1) for x in (core, group, place)]

    def swap(x):
        return lax.ppermute(x, "seq", [(s, s ^ 1) for s in range(length)])

    def along(x, m):
        return lax.ppermute(x, "seq", [(s, s ^ (2 * m)) for s in range(length)])

    def across(x, m):
        if m == 0:
            return x
        return lax.ppermute(x, "grp", [(g, g ^ m) for g in range(groups)])

    def straight(parts):
        moved = []
        for i, x in enumerate(parts):
            side, k = divmod(i, groups)
            if i:
                pairs = [
                    (g * length + s, (g ^ k) * length + (s ^ side))
                    for g in range(groups)
                    for s in range(length)
                ]
                x = lax.ppermute(x, ("grp", "seq"), pairs)
            moved.append(x)
        return moved

    def later(x, m, froms):
        pairs = [(2 * z + c, 2 * (z + m) + c) for z in froms for c in range(2)]
        return lax.ppermute(x, "seq", pairs)

    queries = lin_query.reshape(tokens, -1)
    keys = lin_key.reshape(tokens, -1)
    values = lin_value.reshape(tokens, -1)
    inner = queries.shape[1]
    half = inner // 2

    states = call(
        state_kernel,
        [((inner, HEAD), BF)],
        [pltpu.VMEM(keys.shape, BF)] * 2 + [pltpu.SemaphoreType.DMA((2, 4))],
        away=(0, 1),
    )(keys, values)[0]
    pair = swap(states)
    summed = (states.astype(F32) + pair.astype(F32)).astype(BF)
    summed = lax.dynamic_slice_in_dim(summed, core * half, half, axis=0)
    if stages == 4:
        arrived = [later(summed, 1, range(3)), later(summed, 2, [0])]
        upto = added(summed, arrived[0])
        arrived.append(later(upto, 2, [1]))
    else:
        arrived = [later(summed, m, range(stages - m)) for m in range(1, stages)]

    chosen = expert_ids.reshape(tokens, TOP).T
    scores = route_scores.reshape(tokens, TOP)
    shares = (scores / jnp.sum(scores, axis=1, keepdims=True)).T
    hit = chosen[None] == jnp.arange(expert_count, dtype=jnp.int32)[:, None, None]
    dense = jnp.sum(jnp.where(hit, shares[None], 0.0), axis=1)
    shape = (2 * expert_count, tokens)
    both = call(pack_kernel, [(shape, F32)])(dense, swap(dense))[0]
    packs = [both] + [along(both, m) for m in range(1, stages)]

    inside, out_proj = call(
        inside_kernel,
        [((tokens, inner), F32), (out_proj.shape, BF)],
        [pltpu.VMEM(keys.shape, BF)] * 3
        + [pltpu.SemaphoreType.DMA((3, 4)), pltpu.SemaphoreType.DMA],
        away=(0, 1, 2, 3),
    )(queries, keys, values, out_proj, *scalars)
    shape = (2 * stages * 2 * groups, tokens)
    body = functools.partial(rank_kernel, groups, length)
    routes, ranks = call(body, [(shape, F32)] * 2)(
        *scalars[1:], *packs
    )
    mine = added(*arrived)
    other = swap(mine)
    residual, moe_in = call(
        project_kernel, [((tokens, features), BF)] * 2, [pltpu.VMEM((tokens, inner), BF)]
    )(
        scalars[0],
        inside,
        queries,
        mine,
        other,
        pair,
        lin_gain.reshape(1, inner),
        resid_in.reshape(tokens, features),
        out_proj,
        moe_gain.reshape(1, features),
    )

    routing = sending(stages)
    returning = homing(stages)
    blocks = {0: moe_in}
    outs = {}
    for m in range(1, stages):
        source, shift = routing[m]
        blocks[m] = along(blocks[source], shift)
    for m in range(stages):
        base = m * 2 * groups
        near = m in STRAIGHT_OUT
        partner = None if near else swap(blocks[m])
        if near:
            base += stages * 2 * groups
            picked = straight_select(slots, 2 * groups, base, blocks[m], ranks)
        else:
            picked = select(slots, groups, base, blocks[m], partner, ranks)
        if near:
            taken = straight(picked)
        else:
            taken = [across(picked[k], k) for k in range(groups)]
        outs[m] = experts(
            taken, near, m in STRAIGHT_BACK, groups, gate_weight, up_weight, down_weight
        )
    sums = {m: [] for m in range(stages)}
    sums[0].append(residual)
    for m in back_order(stages):
        base = m * 2 * groups
        if m in STRAIGHT_BACK:
            base += stages * 2 * groups
            backs = straight(outs[m])
            part = straight_combine(slots, base, backs, ranks, routes, sums[m], m == 0)
        else:
            backs = [across(outs[m][k], k) for k in range(groups)]
            own, par = combine(slots, base, backs, ranks, routes)
            part = own.astype(F32) + swap(par).astype(F32)
            for more in sums[m]:
                part = part + more.astype(F32)
            part = part.astype(BF)
        if m:
            into, shift = returning[m]
            sums[into].append(along(part, shift))
    return part.reshape(1, tokens, features)


STRAIGHT_OUT = (0, 1)
STRAIGHT_BACK = (0, 1)


def sending(stages):
    if stages == 4:
        return {1: (0, 1), 2: (0, 2), 3: (2, 1)}
    return {m: (0, m) for m in range(1, stages)}


def homing(stages):
    if stages == 4:
        return {2: (3, 1), 3: (0, 3), 1: (0, 1)}
    return {m: (0, m) for m in range(1, stages)}


def back_order(stages):
    return list(range(2, stages)) + [1, 0]


def solution(mesh):
    rows = P("grp", "seq", None)
    held = P(("grp", "seq"), None, None)
    in_specs = (rows, rows, rows, rows, P(), P(), P(), rows, rows, held, held, held)

    return jax.shard_map(on_device, mesh=mesh, in_specs=in_specs, out_specs=rows, check_vma=False)
```

```python
import functools

import jax
import jax.numpy as jnp
from jax import lax
from jax.experimental import pallas as pl
from jax.experimental.pallas import tpu as pltpu
from jax.sharding import PartitionSpec as P


HEAD = 128
TOP = 8
epsilon = 1e-06
BF = jnp.bfloat16
F32 = jnp.float32


def dot(a, b, ca=1, cb=0):
    return lax.dot_general(a, b, (((ca,), (cb,)), ((), ())), preferred_element_type=F32)


def call(body, outs, scratch=(), limit=24, away=(), leave=False):
    def run(*args):
        specs = []
        placed = []
        for i, x in enumerate(args):
            space = pltpu.SMEM if x.size == 1 else pltpu.VMEM
            if i in away:
                space = pltpu.HBM
            specs.append(pl.BlockSpec(memory_space=space))
            placed.append(pltpu.with_memory_space_constraint(x, space))
        return pl.pallas_call(
            body,
            in_specs=specs,
            out_specs=[pl.BlockSpec(memory_space=pltpu.VMEM)] * len(outs),
            out_shape=[
                jax.ShapeDtypeStruct(shape, dtype) if leave else pltpu.VMEM(shape, dtype)
                for shape, dtype in outs
            ],
            scratch_shapes=list(scratch),
            compiler_params=pltpu.CompilerParams(vmem_limit_bytes=limit << 20),
        )(*placed)

    return run


def column_copies(pairs, sems):
    parts = sems.shape[1]
    copies = []
    for i in range(parts):
        for n, (src, dst) in enumerate(pairs):
            width = dst.shape[1] // parts
            cols = pl.ds(i * width, width)
            copy = pltpu.make_async_copy(src.at[:, cols], dst.at[:, cols], sems.at[n, i])
            copy.start()
            copies.append(copy)

    def wait(i):
        for copy in copies[i * len(pairs) : (i + 1) * len(pairs)]:
            copy.wait()

    return wait


def state_kernel(k_hbm, v_hbm, s_ref, k_ref, v_ref, sems):
    heads = k_ref.shape[1] // HEAD
    parts = sems.shape[1]
    wait = column_copies([(k_hbm, k_ref), (v_hbm, v_ref)], sems)
    for i in range(parts):
        wait(i)
        for h in range(i * heads // parts, (i + 1) * heads // parts):
            cols = slice(h * HEAD, (h + 1) * HEAD)
            s_ref[cols, :] = dot(k_ref[:, cols], v_ref[:, cols], 0, 0).astype(BF)


def inside_kernel(
    q_hbm, k_hbm, v_hbm, w_hbm, core_ref, group_ref, place_ref,
    o_ref, w_ref, q_ref, k_ref, v_ref, sems, w_sem,
):
    tokens = q_ref.shape[0]
    heads = q_ref.shape[1] // HEAD
    parts = sems.shape[1]
    wait = column_copies([(q_hbm, q_ref), (k_hbm, k_ref), (v_hbm, v_ref)], sems)
    bring = pltpu.make_async_copy(w_hbm, w_ref, w_sem)
    bring.start()
    rows = lax.broadcasted_iota(jnp.int32, (tokens, tokens), 0)
    cols = lax.broadcasted_iota(jnp.int32, (tokens, tokens), 1)
    causal = rows >= cols
    for h in range(heads):
        if h % (heads // parts) == 0:
            wait(h // (heads // parts))
        part = slice(h * HEAD, (h + 1) * HEAD)
        scores = dot(q_ref[:, part], k_ref[:, part], 1, 1)
        scores = jnp.where(causal, scores, 0.0).astype(BF)
        o_ref[:, part] = dot(scores, v_ref[:, part])
    bring.wait()


def add_kernel(*refs):
    total = refs[0][...].astype(F32)
    for more in refs[1:-1]:
        total = total + more[...].astype(F32)
    refs[-1][...] = total.astype(BF)


def added(*parts):
    return call(add_kernel, [(parts[0].shape, BF)])(*parts)[0]


def project_kernel(
    core_ref, in_ref, q_ref, mine_ref, other_ref, pair_ref, gain_ref, resid_ref, w_ref, mgain_ref,
    res_ref, moe_ref, normed_ref,
):
    core = core_ref[0]
    heads = q_ref.shape[1] // HEAD
    half = heads // 2
    low = core == 0
    second = jnp.where(low, 0.0, 1.0)
    for h in range(heads):
        part = slice(h * HEAD, (h + 1) * HEAD)
        at = slice((h % half) * HEAD, (h % half + 1) * HEAD)
        first = low if h < half else jnp.logical_not(low)
        prefix = jnp.where(first, mine_ref[at, :].astype(F32), other_ref[at, :].astype(F32))
        carried = (prefix + second * pair_ref[part, :].astype(F32)).astype(BF)
        attended = in_ref[:, part] + dot(q_ref[:, part], carried)
        mean = jnp.mean(attended * attended, axis=1, keepdims=True)
        normed_ref[:, part] = (attended * lax.rsqrt(mean + epsilon) * gain_ref[:, part]).astype(BF)
    features = res_ref.shape[1]
    width = features // 4
    square = jnp.zeros((res_ref.shape[0], 1), F32)
    for i in range(4):
        at = slice(i * width, (i + 1) * width)
        added = resid_ref[:, at].astype(F32) + dot(normed_ref[...], w_ref[:, at])
        rounded = added.astype(BF)
        res_ref[:, at] = rounded
        wide = rounded.astype(F32)
        square = square + jnp.sum(wide * wide, axis=1, keepdims=True)
    scale = lax.rsqrt(square / features + epsilon)
    moe_ref[...] = (res_ref[...].astype(F32) * scale * mgain_ref[...]).astype(BF)


def rank_kernel(groups, length, group_ref, place_ref, *refs):
    tables = refs[:-2]
    route_ref, rank_ref = refs[-2:]
    place = place_ref[0]
    group = group_ref[0]
    row = 0
    for table in tables:
        for side in range(2):
            for k in range(groups):
                at = (group ^ k) * length + (place ^ side)
                route_ref[row : row + 1, :] = table[pl.ds(at, 1), :]
                row += 1
    tokens = route_ref.shape[1]
    rows = lax.broadcasted_iota(jnp.int32, (tokens, tokens), 0)
    cols = lax.broadcasted_iota(jnp.int32, (tokens, tokens), 1)
    earlier = jnp.where(rows < cols, 1.0, 0.0).astype(BF)
    named = route_ref[...] > 0.0
    rank = dot(jnp.where(named, 1.0, 0.0).astype(BF), earlier)
    rank_ref[...] = jnp.where(named, rank, -1.0)


def slots_of(rank_ref, value, row, slots):
    rank = rank_ref[row : row + 1, :]
    number = lax.broadcasted_iota(jnp.int32, (slots, rank.shape[1]), 0).astype(F32)
    return jnp.where(number == rank, value, 0.0)


def select_kernel(slots, base, own_ref, rank_ref, *outs):
    rows = [slots_of(rank_ref, 1.0, base + i, slots) for i in range(len(outs))]
    picked = dot(jnp.concatenate(rows, axis=0).astype(BF), own_ref[...]).astype(BF)
    for i, out in enumerate(outs):
        out[...] = picked[i * slots : (i + 1) * slots]


def select(slots, count, base, own, rank):
    body = functools.partial(select_kernel, slots, base)
    shape = ((slots, own.shape[1]), BF)
    return call(body, [shape] * count)(own, rank)


def combine_kernel(slots, count, base, *refs):
    backs = refs[:count]
    rank_ref, weight_ref = refs[count : count + 2]
    more = refs[count + 2 : -1]
    rows = stacked(backs)
    parts = []
    for i in range(count):
        row = base + i
        parts.append(slots_of(rank_ref, weight_ref[row : row + 1, :], row, slots))
    total = dot(jnp.concatenate(parts, axis=0).astype(BF), rows, 0, 0)
    for ref in more:
        total = total + ref[...].astype(F32)
    refs[-1][...] = total.astype(BF)


def combine(slots, base, backs, rank, weight, more, leave):
    body = functools.partial(combine_kernel, slots, len(backs), base)
    shape = ((rank.shape[1], backs[0].shape[1]), BF)
    return call(body, [shape], leave=leave)(*backs, rank, weight, *more)[0]


def stacked(refs):
    if refs[0].shape[0] % 16 == 0:
        return jnp.concatenate([r[...] for r in refs], axis=0)
    return jnp.concatenate([r[...].astype(F32) for r in refs], axis=0).astype(BF)


def expert_kernel(count, *refs):
    xs = refs[:count]
    gate_ref, up_ref, down_ref = refs[count : count + 3]
    outs = refs[count + 3 : -1]
    hidden_ref = refs[-1]
    slots, features = xs[0].shape
    units = gate_ref.shape[2]
    x = stacked(xs)
    width = 256
    for j in range(units // width):
        at = slice(j * width, (j + 1) * width)
        gate = dot(x, gate_ref[0, :, at])
        up = dot(x, up_ref[0, :, at])
        hidden_ref[:, at] = (gate / (1.0 + jnp.exp(-gate)) * up).astype(BF)
    hidden = hidden_ref[...]
    width = 512
    for j in range(features // width):
        at = slice(j * width, (j + 1) * width)
        out = dot(hidden, down_ref[0, :, at])
        for i, ref in enumerate(outs):
            ref[:, at] = out[i * slots : (i + 1) * slots].astype(BF)


def experts(xs, gate, up, down):
    body = functools.partial(expert_kernel, len(xs))
    scratch = [pltpu.VMEM((sum(x.shape[0] for x in xs), gate.shape[2]), BF)]
    outs = [(xs[0].shape, BF)] * len(xs)
    return call(body, outs, scratch)(*xs, gate, up, down)


def on_device(
    resid_in,
    lin_query,
    lin_key,
    lin_value,
    lin_gain,
    out_proj,
    moe_gain,
    expert_ids,
    route_scores,
    gate_weight,
    up_weight,
    down_weight,
):
    tokens = resid_in.shape[1]
    features = resid_in.shape[2]
    groups = lax.axis_size("grp")
    length = lax.axis_size("seq")
    stages = length // 2
    group = lax.axis_index("grp")
    place = lax.axis_index("seq")
    core = place % 2
    expert_count = gate_weight.shape[0] * groups * length
    capacity = tokens * TOP * 5 // (4 * expert_count)
    slots = -(-capacity // 8) * 8

    scalars = [x.reshape(1) for x in (core, group, place)]

    def swap(x):
        return lax.ppermute(x, "seq", [(s, s ^ 1) for s in range(length)])

    def along(x, m):
        return lax.ppermute(x, "seq", [(s, s ^ (2 * m)) for s in range(length)])

    def straight(parts):
        moved = []
        for i, x in enumerate(parts):
            side, k = divmod(i, groups)
            if i:
                pairs = [
                    (g * length + s, (g ^ k) * length + (s ^ side))
                    for g in range(groups)
                    for s in range(length)
                ]
                x = lax.ppermute(x, ("grp", "seq"), pairs)
            moved.append(x)
        return moved

    def later(x, m, froms):
        pairs = [(2 * z + c, 2 * (z + m) + c) for z in froms for c in range(2)]
        return lax.ppermute(x, "seq", pairs)

    queries = lin_query.reshape(tokens, -1)
    keys = lin_key.reshape(tokens, -1)
    values = lin_value.reshape(tokens, -1)
    inner = queries.shape[1]
    half = inner // 2

    states = call(
        state_kernel,
        [((inner, HEAD), BF)],
        [pltpu.VMEM(keys.shape, BF)] * 2 + [pltpu.SemaphoreType.DMA((2, 4))],
        away=(0, 1),
    )(keys, values)[0]
    pair = swap(states)
    summed = (states.astype(F32) + pair.astype(F32)).astype(BF)
    summed = lax.dynamic_slice_in_dim(summed, core * half, half, axis=0)
    if stages == 4:
        arrived = [later(summed, 1, range(3)), later(summed, 2, [0])]
        upto = added(summed, arrived[0])
        arrived.append(later(upto, 2, [1]))
    else:
        arrived = [later(summed, m, range(stages - m)) for m in range(1, stages)]

    chosen = expert_ids.reshape(tokens, TOP).T
    scores = route_scores.reshape(tokens, TOP)
    shares = (scores / jnp.sum(scores, axis=1, keepdims=True)).T
    hit = chosen[None] == jnp.arange(expert_count, dtype=jnp.int32)[:, None, None]
    dense = jnp.sum(jnp.where(hit, shares[None], 0.0), axis=1)
    tables = [dense] + [along(dense, m) for m in range(1, stages)]

    inside, out_proj = call(
        inside_kernel,
        [((tokens, inner), F32), (out_proj.shape, BF)],
        [pltpu.VMEM(keys.shape, BF)] * 3
        + [pltpu.SemaphoreType.DMA((3, 4)), pltpu.SemaphoreType.DMA],
        away=(0, 1, 2, 3),
    )(queries, keys, values, out_proj, *scalars)
    shape = (stages * 2 * groups, tokens)
    body = functools.partial(rank_kernel, groups, length)
    routes, ranks = call(body, [(shape, F32)] * 2)(
        *scalars[1:], *tables
    )
    mine = added(*arrived)
    other = swap(mine)
    residual, moe_in = call(
        project_kernel, [((tokens, features), BF)] * 2, [pltpu.VMEM((tokens, inner), BF)]
    )(
        scalars[0],
        inside,
        queries,
        mine,
        other,
        pair,
        lin_gain.reshape(1, inner),
        resid_in.reshape(tokens, features),
        out_proj,
        moe_gain.reshape(1, features),
    )

    routing = sending(stages)
    returning = homing(stages)
    blocks = {0: moe_in}
    outs = {}
    for m in range(1, stages):
        source, shift = routing[m]
        blocks[m] = along(blocks[source], shift)
    for m in range(stages):
        base = m * 2 * groups
        picked = select(slots, 2 * groups, base, blocks[m], ranks)
        taken = straight(picked)
        outs[m] = experts(taken, gate_weight, up_weight, down_weight)
    sums = {m: [] for m in range(stages)}
    sums[0].append(residual)
    for m in back_order(stages):
        base = m * 2 * groups
        backs = straight(outs[m])
        part = combine(slots, base, backs, ranks, routes, sums[m], m == 0)
        if m:
            into, shift = returning[m]
            sums[into].append(along(part, shift))
    return part.reshape(1, tokens, features)


def sending(stages):
    if stages == 4:
        return {1: (0, 1), 2: (0, 2), 3: (2, 1)}
    return {m: (0, m) for m in range(1, stages)}


def homing(stages):
    if stages == 4:
        return {2: (3, 1), 3: (0, 3), 1: (0, 1)}
    return {m: (0, m) for m in range(1, stages)}


def back_order(stages):
    return list(range(2, stages)) + [1, 0]


def solution(mesh):
    rows = P("grp", "seq", None)
    held = P(("grp", "seq"), None, None)
    in_specs = (rows, rows, rows, rows, P(), P(), P(), rows, rows, held, held, held)

    return jax.shard_map(on_device, mesh=mesh, in_specs=in_specs, out_specs=rows, check_vma=False)
```

```python
import functools

import jax
import jax.numpy as jnp
from jax import lax
from jax.experimental import pallas as pl
from jax.experimental.pallas import tpu as pltpu
from jax.sharding import PartitionSpec as P


HEAD = 128
TOP = 8
epsilon = 1e-06
BF = jnp.bfloat16
F32 = jnp.float32


def dot(a, b, ca=1, cb=0):
    return lax.dot_general(a, b, (((ca,), (cb,)), ((), ())), preferred_element_type=F32)


def call(body, outs, scratch=(), limit=24, away=(), leave=False):
    def run(*args):
        specs = []
        placed = []
        for i, x in enumerate(args):
            space = pltpu.SMEM if x.size == 1 else pltpu.VMEM
            if i in away:
                space = pltpu.HBM
            specs.append(pl.BlockSpec(memory_space=space))
            placed.append(pltpu.with_memory_space_constraint(x, space))
        return pl.pallas_call(
            body,
            in_specs=specs,
            out_specs=[pl.BlockSpec(memory_space=pltpu.VMEM)] * len(outs),
            out_shape=[
                jax.ShapeDtypeStruct(shape, dtype) if leave else pltpu.VMEM(shape, dtype)
                for shape, dtype in outs
            ],
            scratch_shapes=list(scratch),
            compiler_params=pltpu.CompilerParams(vmem_limit_bytes=limit << 20),
        )(*placed)

    return run


def column_copies(pairs, sems):
    parts = sems.shape[1]
    copies = []
    for i in range(parts):
        for n, (src, dst) in enumerate(pairs):
            width = dst.shape[1] // parts
            cols = pl.ds(i * width, width)
            copy = pltpu.make_async_copy(src.at[:, cols], dst.at[:, cols], sems.at[n, i])
            copy.start()
            copies.append(copy)

    def wait(i):
        for copy in copies[i * len(pairs) : (i + 1) * len(pairs)]:
            copy.wait()

    return wait


def state_kernel(k_hbm, v_hbm, s_ref, k_ref, v_ref, sems):
    heads = k_ref.shape[1] // HEAD
    parts = sems.shape[1]
    wait = column_copies([(k_hbm, k_ref), (v_hbm, v_ref)], sems)
    for i in range(parts):
        wait(i)
        for h in range(i * heads // parts, (i + 1) * heads // parts):
            cols = slice(h * HEAD, (h + 1) * HEAD)
            s_ref[cols, :] = dot(k_ref[:, cols], v_ref[:, cols], 0, 0).astype(BF)


def inside_kernel(
    q_hbm, k_hbm, v_hbm, w_hbm, core_ref, group_ref, place_ref,
    o_ref, w_ref, q_ref, k_ref, v_ref, sems, w_sem,
):
    tokens = q_ref.shape[0]
    heads = q_ref.shape[1] // HEAD
    parts = sems.shape[1]
    wait = column_copies([(q_hbm, q_ref), (k_hbm, k_ref), (v_hbm, v_ref)], sems)
    bring = pltpu.make_async_copy(w_hbm, w_ref, w_sem)
    bring.start()
    rows = lax.broadcasted_iota(jnp.int32, (tokens, tokens), 0)
    cols = lax.broadcasted_iota(jnp.int32, (tokens, tokens), 1)
    causal = rows >= cols
    for h in range(heads):
        if h % (heads // parts) == 0:
            wait(h // (heads // parts))
        part = slice(h * HEAD, (h + 1) * HEAD)
        scores = dot(q_ref[:, part], k_ref[:, part], 1, 1)
        scores = jnp.where(causal, scores, 0.0).astype(BF)
        o_ref[:, part] = dot(scores, v_ref[:, part])
    bring.wait()


def add_kernel(*refs):
    total = refs[0][...].astype(F32)
    for more in refs[1:-1]:
        total = total + more[...].astype(F32)
    refs[-1][...] = total.astype(BF)


def added(*parts):
    return call(add_kernel, [(parts[0].shape, BF)])(*parts)[0]


def project_kernel(
    core_ref, in_ref, q_ref, mine_ref, other_ref, pair_ref, gain_ref, resid_ref, w_ref, mgain_ref,
    res_ref, moe_ref, normed_ref,
):
    core = core_ref[0]
    heads = q_ref.shape[1] // HEAD
    half = heads // 2
    low = core == 0
    second = jnp.where(low, 0.0, 1.0)
    for h in range(heads):
        part = slice(h * HEAD, (h + 1) * HEAD)
        at = slice((h % half) * HEAD, (h % half + 1) * HEAD)
        first = low if h < half else jnp.logical_not(low)
        prefix = jnp.where(first, mine_ref[at, :].astype(F32), other_ref[at, :].astype(F32))
        carried = (prefix + second * pair_ref[part, :].astype(F32)).astype(BF)
        attended = in_ref[:, part] + dot(q_ref[:, part], carried)
        mean = jnp.mean(attended * attended, axis=1, keepdims=True)
        normed_ref[:, part] = (attended * lax.rsqrt(mean + epsilon) * gain_ref[:, part]).astype(BF)
    features = res_ref.shape[1]
    width = features // 4
    square = jnp.zeros((res_ref.shape[0], 1), F32)
    for i in range(4):
        at = slice(i * width, (i + 1) * width)
        added = resid_ref[:, at].astype(F32) + dot(normed_ref[...], w_ref[:, at])
        rounded = added.astype(BF)
        res_ref[:, at] = rounded
        wide = rounded.astype(F32)
        square = square + jnp.sum(wide * wide, axis=1, keepdims=True)
    scale = lax.rsqrt(square / features + epsilon)
    moe_ref[...] = (res_ref[...].astype(F32) * scale * mgain_ref[...]).astype(BF)


def rank_kernel(groups, length, group_ref, place_ref, *refs):
    tables = refs[:-2]
    route_ref, rank_ref = refs[-2:]
    place = place_ref[0]
    group = group_ref[0]
    row = 0
    for table in tables:
        for side in range(2):
            for k in range(groups):
                at = (group ^ k) * length + (place ^ side)
                route_ref[row : row + 1, :] = table[pl.ds(at, 1), :]
                row += 1
    tokens = route_ref.shape[1]
    rows = lax.broadcasted_iota(jnp.int32, (tokens, tokens), 0)
    cols = lax.broadcasted_iota(jnp.int32, (tokens, tokens), 1)
    earlier = jnp.where(rows < cols, 1.0, 0.0).astype(BF)
    named = route_ref[...] > 0.0
    rank = dot(jnp.where(named, 1.0, 0.0).astype(BF), earlier)
    rank_ref[...] = jnp.where(named, rank, -1.0)


def slots_of(rank_ref, value, row, slots):
    rank = rank_ref[row : row + 1, :]
    number = lax.broadcasted_iota(jnp.int32, (slots, rank.shape[1]), 0).astype(F32)
    return jnp.where(number == rank, value, 0.0)


def select_kernel(slots, base, own_ref, rank_ref, *outs):
    rows = [slots_of(rank_ref, 1.0, base + i, slots) for i in range(len(outs))]
    picked = dot(jnp.concatenate(rows, axis=0).astype(BF), own_ref[...]).astype(BF)
    for i, out in enumerate(outs):
        out[...] = picked[i * slots : (i + 1) * slots]


def select(slots, count, base, own, rank):
    body = functools.partial(select_kernel, slots, base)
    shape = ((slots, own.shape[1]), BF)
    return call(body, [shape] * count)(own, rank)


def combine_kernel(slots, count, base, *refs):
    backs = refs[:count]
    rank_ref, weight_ref = refs[count : count + 2]
    more = refs[count + 2 : -1]
    rows = stacked(backs)
    parts = []
    for i in range(count):
        row = base + i
        parts.append(slots_of(rank_ref, weight_ref[row : row + 1, :], row, slots))
    total = dot(jnp.concatenate(parts, axis=0).astype(BF), rows, 0, 0)
    for ref in more:
        total = total + ref[...].astype(F32)
    refs[-1][...] = total.astype(BF)


def combine(slots, base, backs, rank, weight, more, leave):
    body = functools.partial(combine_kernel, slots, len(backs), base)
    shape = ((rank.shape[1], backs[0].shape[1]), BF)
    return call(body, [shape], leave=leave)(*backs, rank, weight, *more)[0]


def stacked(refs):
    if refs[0].shape[0] % 16 == 0:
        return jnp.concatenate([r[...] for r in refs], axis=0)
    return jnp.concatenate([r[...].astype(F32) for r in refs], axis=0).astype(BF)


def expert_kernel(count, *refs):
    xs = refs[:count]
    gate_ref, up_ref, down_ref = refs[count : count + 3]
    outs = refs[count + 3 : -1]
    hidden_ref = refs[-1]
    slots, features = xs[0].shape
    units = gate_ref.shape[2]
    x = stacked(xs)
    width = 256
    for j in range(units // width):
        at = slice(j * width, (j + 1) * width)
        gate = dot(x, gate_ref[0, :, at])
        up = dot(x, up_ref[0, :, at])
        hidden_ref[:, at] = (gate / (1.0 + jnp.exp(-gate)) * up).astype(BF)
    hidden = hidden_ref[...]
    width = 512
    for j in range(features // width):
        at = slice(j * width, (j + 1) * width)
        out = dot(hidden, down_ref[0, :, at])
        for i, ref in enumerate(outs):
            ref[:, at] = out[i * slots : (i + 1) * slots].astype(BF)


def experts(xs, gate, up, down):
    body = functools.partial(expert_kernel, len(xs))
    scratch = [pltpu.VMEM((sum(x.shape[0] for x in xs), gate.shape[2]), BF)]
    outs = [(xs[0].shape, BF)] * len(xs)
    return call(body, outs, scratch)(*xs, gate, up, down)


def on_device(
    resid_in,
    lin_query,
    lin_key,
    lin_value,
    lin_gain,
    out_proj,
    moe_gain,
    expert_ids,
    route_scores,
    gate_weight,
    up_weight,
    down_weight,
):
    tokens = resid_in.shape[1]
    features = resid_in.shape[2]
    groups = lax.axis_size("grp")
    length = lax.axis_size("seq")
    stages = length // 2
    group = lax.axis_index("grp")
    place = lax.axis_index("seq")
    core = place % 2
    expert_count = gate_weight.shape[0] * groups * length
    capacity = tokens * TOP * 5 // (4 * expert_count)
    slots = -(-capacity // 8) * 8

    scalars = [x.reshape(1) for x in (core, group, place)]

    def swap(x):
        return lax.ppermute(x, "seq", [(s, s ^ 1) for s in range(length)])

    def along(x, m):
        return lax.ppermute(x, "seq", [(s, s ^ (2 * m)) for s in range(length)])

    def straight(parts):
        moved = []
        for i, x in enumerate(parts):
            side, k = divmod(i, groups)
            if i:
                pairs = [
                    (g * length + s, (g ^ k) * length + (s ^ side))
                    for g in range(groups)
                    for s in range(length)
                ]
                x = lax.ppermute(x, ("grp", "seq"), pairs)
            moved.append(x)
        return moved

    def later(x, m, froms):
        pairs = [(2 * z + c, 2 * (z + m) + c) for z in froms for c in range(2)]
        return lax.ppermute(x, "seq", pairs)

    queries = lin_query.reshape(tokens, -1)
    keys = lin_key.reshape(tokens, -1)
    values = lin_value.reshape(tokens, -1)
    inner = queries.shape[1]
    half = inner // 2

    states = call(
        state_kernel,
        [((inner, HEAD), BF)],
        [pltpu.VMEM(keys.shape, BF)] * 2 + [pltpu.SemaphoreType.DMA((2, 4))],
        away=(0, 1),
    )(keys, values)[0]
    pair = swap(states)
    summed = (states.astype(F32) + pair.astype(F32)).astype(BF)
    summed = lax.dynamic_slice_in_dim(summed, core * half, half, axis=0)
    if stages == 4:
        arrived = [later(summed, 1, range(3)), later(summed, 2, [0])]
        upto = added(summed, arrived[0])
        arrived.append(later(upto, 2, [1]))
    else:
        arrived = [later(summed, m, range(stages - m)) for m in range(1, stages)]

    chosen = expert_ids.reshape(tokens, TOP).T
    scores = route_scores.reshape(tokens, TOP)
    shares = (scores / jnp.sum(scores, axis=1, keepdims=True)).T
    hit = chosen[None] == jnp.arange(expert_count, dtype=jnp.int32)[:, None, None]
    dense = jnp.sum(jnp.where(hit, shares[None], 0.0), axis=1)
    tables = [dense] + [along(dense, m) for m in range(1, stages)]

    inside, out_proj = call(
        inside_kernel,
        [((tokens, inner), F32), (out_proj.shape, BF)],
        [pltpu.VMEM(keys.shape, BF)] * 3
        + [pltpu.SemaphoreType.DMA((3, 4)), pltpu.SemaphoreType.DMA],
        away=(0, 1, 2, 3),
    )(queries, keys, values, out_proj, *scalars)

    def ranked(held):
        shape = (len(held) * 2 * groups, tokens)
        body = functools.partial(rank_kernel, groups, length)
        return call(body, [(shape, F32)] * 2)(*scalars[1:], *held)

    own_tables = ranked(tables[:1])
    rest_tables = ranked(tables[1:])
    lookup = {m: (rest_tables, (m - 1) * 2 * groups) for m in range(1, stages)}
    lookup[0] = (own_tables, 0)

    mine = added(*arrived)
    other = swap(mine)
    residual, moe_in = call(
        project_kernel, [((tokens, features), BF)] * 2, [pltpu.VMEM((tokens, inner), BF)]
    )(
        scalars[0],
        inside,
        queries,
        mine,
        other,
        pair,
        lin_gain.reshape(1, inner),
        resid_in.reshape(tokens, features),
        out_proj,
        moe_gain.reshape(1, features),
    )

    routing = sending(stages)
    returning = homing(stages)
    blocks = {0: moe_in}
    outs = {}
    for m in range(1, stages):
        source, shift = routing[m]
        blocks[m] = along(blocks[source], shift)
    for m in range(stages):
        (routes, ranks), base = lookup[m]
        picked = select(slots, 2 * groups, base, blocks[m], ranks)
        taken = straight(picked)
        outs[m] = experts(taken, gate_weight, up_weight, down_weight)
    sums = {m: [] for m in range(stages)}
    sums[0].append(residual)
    for m in back_order(stages):
        (routes, ranks), base = lookup[m]
        backs = straight(outs[m])
        part = combine(slots, base, backs, ranks, routes, sums[m], m == 0)
        if m:
            into, shift = returning[m]
            sums[into].append(along(part, shift))
    return part.reshape(1, tokens, features)


def sending(stages):
    if stages == 4:
        return {1: (0, 1), 2: (0, 2), 3: (2, 1)}
    return {m: (0, m) for m in range(1, stages)}


def homing(stages):
    if stages == 4:
        return {2: (3, 1), 3: (0, 3), 1: (0, 1)}
    return {m: (0, m) for m in range(1, stages)}


def back_order(stages):
    return list(range(2, stages)) + [1, 0]


def solution(mesh):
    rows = P("grp", "seq", None)
    held = P(("grp", "seq"), None, None)
    in_specs = (rows, rows, rows, rows, P(), P(), P(), rows, rows, held, held, held)

    return jax.shard_map(on_device, mesh=mesh, in_specs=in_specs, out_specs=rows, check_vma=False)
```

```python
import functools

import jax
import jax.numpy as jnp
from jax import lax
from jax.experimental import pallas as pl
from jax.experimental.pallas import tpu as pltpu
from jax.sharding import PartitionSpec as P


HEAD = 128
TOP = 8
epsilon = 1e-06
BF = jnp.bfloat16
F32 = jnp.float32


def dot(a, b, ca=1, cb=0):
    return lax.dot_general(a, b, (((ca,), (cb,)), ((), ())), preferred_element_type=F32)


def call(body, outs, scratch=(), limit=24, away=(), leave=False):
    def run(*args):
        specs = []
        placed = []
        for i, x in enumerate(args):
            space = pltpu.SMEM if x.size == 1 else pltpu.VMEM
            if i in away:
                space = pltpu.HBM
            specs.append(pl.BlockSpec(memory_space=space))
            placed.append(pltpu.with_memory_space_constraint(x, space))
        return pl.pallas_call(
            body,
            in_specs=specs,
            out_specs=[pl.BlockSpec(memory_space=pltpu.HBM if leave else pltpu.VMEM)] * len(outs),
            out_shape=[
                jax.ShapeDtypeStruct(shape, dtype) if leave else pltpu.VMEM(shape, dtype)
                for shape, dtype in outs
            ],
            scratch_shapes=list(scratch),
            compiler_params=pltpu.CompilerParams(vmem_limit_bytes=limit << 20),
        )(*placed)

    return run


def column_copies(pairs, sems):
    parts = sems.shape[1]
    copies = []
    for i in range(parts):
        for n, (src, dst) in enumerate(pairs):
            width = dst.shape[1] // parts
            cols = pl.ds(i * width, width)
            copy = pltpu.make_async_copy(src.at[:, cols], dst.at[:, cols], sems.at[n, i])
            copy.start()
            copies.append(copy)

    def wait(i):
        for copy in copies[i * len(pairs) : (i + 1) * len(pairs)]:
            copy.wait()

    return wait


def state_kernel(k_hbm, v_hbm, s_ref, k_ref, v_ref, sems):
    heads = k_ref.shape[1] // HEAD
    parts = sems.shape[1]
    wait = column_copies([(k_hbm, k_ref), (v_hbm, v_ref)], sems)
    for i in range(parts):
        wait(i)
        for h in range(i * heads // parts, (i + 1) * heads // parts):
            cols = slice(h * HEAD, (h + 1) * HEAD)
            s_ref[cols, :] = dot(k_ref[:, cols], v_ref[:, cols], 0, 0).astype(BF)


def inside_kernel(
    q_hbm, k_hbm, v_hbm, w_hbm, core_ref, group_ref, place_ref,
    o_ref, w_ref, q_ref, k_ref, v_ref, sems, w_sem,
):
    tokens = q_ref.shape[0]
    heads = q_ref.shape[1] // HEAD
    parts = sems.shape[1]
    wait = column_copies([(q_hbm, q_ref), (k_hbm, k_ref), (v_hbm, v_ref)], sems)
    bring = pltpu.make_async_copy(w_hbm, w_ref, w_sem)
    bring.start()
    rows = lax.broadcasted_iota(jnp.int32, (tokens, tokens), 0)
    cols = lax.broadcasted_iota(jnp.int32, (tokens, tokens), 1)
    causal = rows >= cols
    for h in range(heads):
        if h % (heads // parts) == 0:
            wait(h // (heads // parts))
        part = slice(h * HEAD, (h + 1) * HEAD)
        scores = dot(q_ref[:, part], k_ref[:, part], 1, 1)
        scores = jnp.where(causal, scores, 0.0).astype(BF)
        o_ref[:, part] = dot(scores, v_ref[:, part])
    bring.wait()


def add_kernel(*refs):
    total = refs[0][...].astype(F32)
    for more in refs[1:-1]:
        total = total + more[...].astype(F32)
    refs[-1][...] = total.astype(BF)


def added(*parts):
    return call(add_kernel, [(parts[0].shape, BF)])(*parts)[0]


def project_kernel(
    slots, core_ref, in_ref, q_ref, mine_ref, other_ref, pair_ref, gain_ref, resid_ref, w_ref,
    mgain_ref, rank_ref, res_ref, moe_ref, *rest,
):
    outs, normed_ref = rest[:-1], rest[-1]
    pick = picks(slots, rank_ref, 0, len(outs))
    core = core_ref[0]
    heads = q_ref.shape[1] // HEAD
    half = heads // 2
    low = core == 0
    second = jnp.where(low, 0.0, 1.0)
    for h in range(heads):
        part = slice(h * HEAD, (h + 1) * HEAD)
        at = slice((h % half) * HEAD, (h % half + 1) * HEAD)
        first = low if h < half else jnp.logical_not(low)
        prefix = jnp.where(first, mine_ref[at, :].astype(F32), other_ref[at, :].astype(F32))
        carried = (prefix + second * pair_ref[part, :].astype(F32)).astype(BF)
        attended = in_ref[:, part] + dot(q_ref[:, part], carried)
        mean = jnp.mean(attended * attended, axis=1, keepdims=True)
        normed_ref[:, part] = (attended * lax.rsqrt(mean + epsilon) * gain_ref[:, part]).astype(BF)
    features = res_ref.shape[1]
    width = features // 4
    square = jnp.zeros((res_ref.shape[0], 1), F32)
    for i in range(4):
        at = slice(i * width, (i + 1) * width)
        added = resid_ref[:, at].astype(F32) + dot(normed_ref[...], w_ref[:, at])
        rounded = added.astype(BF)
        res_ref[:, at] = rounded
        wide = rounded.astype(F32)
        square = square + jnp.sum(wide * wide, axis=1, keepdims=True)
    scale = lax.rsqrt(square / features + epsilon)
    for i in range(4):
        at = slice(i * width, (i + 1) * width)
        moe_in = (res_ref[:, at].astype(F32) * scale * mgain_ref[:, at]).astype(BF)
        moe_ref[:, at] = moe_in
        picked = dot(pick, moe_in)
        for k, out in enumerate(outs):
            out[:, at] = picked[k * slots : (k + 1) * slots].astype(BF)


def rank_kernel(groups, length, group_ref, place_ref, *refs):
    tables = refs[:-2]
    route_ref, rank_ref = refs[-2:]
    place = place_ref[0]
    group = group_ref[0]
    row = 0
    for table in tables:
        for side in range(2):
            for k in range(groups):
                at = (group ^ k) * length + (place ^ side)
                route_ref[row : row + 1, :] = table[pl.ds(at, 1), :]
                row += 1
    tokens = route_ref.shape[1]
    rows = lax.broadcasted_iota(jnp.int32, (tokens, tokens), 0)
    cols = lax.broadcasted_iota(jnp.int32, (tokens, tokens), 1)
    earlier = jnp.where(rows < cols, 1.0, 0.0).astype(BF)
    named = route_ref[...] > 0.0
    rank = dot(jnp.where(named, 1.0, 0.0).astype(BF), earlier)
    rank_ref[...] = jnp.where(named, rank, -1.0)


def slots_of(rank_ref, value, row, slots):
    rank = rank_ref[row : row + 1, :]
    number = lax.broadcasted_iota(jnp.int32, (slots, rank.shape[1]), 0).astype(F32)
    return jnp.where(number == rank, value, 0.0)


def picks(slots, rank_ref, base, count):
    rows = [slots_of(rank_ref, 1.0, base + i, slots) for i in range(count)]
    return jnp.concatenate(rows, axis=0).astype(BF)


def select_kernel(slots, base, own_ref, rank_ref, *outs):
    picked = dot(picks(slots, rank_ref, base, len(outs)), own_ref[...]).astype(BF)
    for i, out in enumerate(outs):
        out[...] = picked[i * slots : (i + 1) * slots]


def select(slots, count, base, own, rank):
    body = functools.partial(select_kernel, slots, base)
    shape = ((slots, own.shape[1]), BF)
    return call(body, [shape] * count)(own, rank)


def combine_kernel(slots, count, base, *refs):
    backs = refs[:count]
    rank_ref, weight_ref = refs[count : count + 2]
    more = refs[count + 2 : -1]
    rows = stacked(backs)
    total = dot(shares_of(slots, count, base, rank_ref, weight_ref), rows, 0, 0)
    for ref in more:
        total = total + ref[...].astype(F32)
    refs[-1][...] = total.astype(BF)


def finish_kernel(slots, count, base, *refs):
    backs = refs[:count]
    rank_ref, weight_ref = refs[count : count + 2]
    more = refs[count + 2 : -3]
    out_hbm, out_ref, sems = refs[-3:]
    shares = shares_of(slots, count, base, rank_ref, weight_ref)
    parts = sems.shape[0]
    width = out_ref.shape[1] // parts
    copies = []
    for i in range(parts):
        at = pl.ds(i * width, width)
        total = dot(shares, stacked([r.at[:, at] for r in backs]), 0, 0)
        for ref in more:
            total = total + ref[:, at].astype(F32)
        out_ref[:, at] = total.astype(BF)
        copies.append(pltpu.make_async_copy(out_ref.at[:, at], out_hbm.at[:, at], sems.at[i]))
        copies[-1].start()
    for copy in copies:
        copy.wait()


def shares_of(slots, count, base, rank_ref, weight_ref):
    parts = []
    for row in range(base, base + count):
        parts.append(slots_of(rank_ref, weight_ref[row : row + 1, :], row, slots))
    return jnp.concatenate(parts, axis=0).astype(BF)


def combine(slots, base, backs, rank, weight, more, last):
    shape = ((rank.shape[1], backs[0].shape[1]), BF)
    kernel, scratch = combine_kernel, []
    if last:
        kernel = finish_kernel
        scratch = [pltpu.VMEM(*shape), pltpu.SemaphoreType.DMA((4,))]
    body = functools.partial(kernel, slots, len(backs), base)
    return call(body, [shape], scratch, leave=last)(*backs, rank, weight, *more)[0]


def stacked(refs):
    if refs[0].shape[0] % 16 == 0:
        return jnp.concatenate([r[...] for r in refs], axis=0)
    return jnp.concatenate([r[...].astype(F32) for r in refs], axis=0).astype(BF)


def expert_kernel(count, *refs):
    xs = refs[:count]
    gate_ref, up_ref, down_ref = refs[count : count + 3]
    outs = refs[count + 3 : -1]
    hidden_ref = refs[-1]
    slots, features = xs[0].shape
    units = gate_ref.shape[2]
    x = stacked(xs)
    width = 256
    for j in range(units // width):
        at = slice(j * width, (j + 1) * width)
        gate = dot(x, gate_ref[0, :, at])
        up = dot(x, up_ref[0, :, at])
        hidden_ref[:, at] = (gate / (1.0 + jnp.exp(-gate)) * up).astype(BF)
    hidden = hidden_ref[...]
    width = 512
    for j in range(features // width):
        at = slice(j * width, (j + 1) * width)
        out = dot(hidden, down_ref[0, :, at])
        for i, ref in enumerate(outs):
            ref[:, at] = out[i * slots : (i + 1) * slots].astype(BF)


def experts(xs, gate, up, down):
    body = functools.partial(expert_kernel, len(xs))
    scratch = [pltpu.VMEM((sum(x.shape[0] for x in xs), gate.shape[2]), BF)]
    outs = [(xs[0].shape, BF)] * len(xs)
    return call(body, outs, scratch)(*xs, gate, up, down)


def on_device(
    resid_in,
    lin_query,
    lin_key,
    lin_value,
    lin_gain,
    out_proj,
    moe_gain,
    expert_ids,
    route_scores,
    gate_weight,
    up_weight,
    down_weight,
):
    tokens = resid_in.shape[1]
    features = resid_in.shape[2]
    groups = lax.axis_size("grp")
    length = lax.axis_size("seq")
    stages = length // 2
    group = lax.axis_index("grp")
    place = lax.axis_index("seq")
    core = place % 2
    expert_count = gate_weight.shape[0] * groups * length
    capacity = tokens * TOP * 5 // (4 * expert_count)
    slots = -(-capacity // 8) * 8

    scalars = [x.reshape(1) for x in (core, group, place)]

    def swap(x):
        return lax.ppermute(x, "seq", [(s, s ^ 1) for s in range(length)])

    def along(x, m):
        return lax.ppermute(x, "seq", [(s, s ^ (2 * m)) for s in range(length)])

    def straight(parts):
        moved = []
        for i, x in enumerate(parts):
            side, k = divmod(i, groups)
            if i:
                pairs = [
                    (g * length + s, (g ^ k) * length + (s ^ side))
                    for g in range(groups)
                    for s in range(length)
                ]
                x = lax.ppermute(x, ("grp", "seq"), pairs)
            moved.append(x)
        return moved

    def later(x, m, froms):
        pairs = [(2 * z + c, 2 * (z + m) + c) for z in froms for c in range(2)]
        return lax.ppermute(x, "seq", pairs)

    queries = lin_query.reshape(tokens, -1)
    keys = lin_key.reshape(tokens, -1)
    values = lin_value.reshape(tokens, -1)
    inner = queries.shape[1]
    half = inner // 2

    states = call(
        state_kernel,
        [((inner, HEAD), BF)],
        [pltpu.VMEM(keys.shape, BF)] * 2 + [pltpu.SemaphoreType.DMA((2, 1))],
        away=(0, 1),
    )(keys, values)[0]
    pair = swap(states)
    summed = (states.astype(F32) + pair.astype(F32)).astype(BF)
    summed = lax.dynamic_slice_in_dim(summed, core * half, half, axis=0)
    if stages == 4:
        arrived = [later(summed, 1, range(3)), later(summed, 2, [0])]
        upto = added(summed, arrived[0])
        arrived.append(later(upto, 2, [1]))
    else:
        arrived = [later(summed, m, range(stages - m)) for m in range(1, stages)]

    chosen = expert_ids.reshape(tokens, TOP).T
    scores = route_scores.reshape(tokens, TOP)
    shares = (scores / jnp.sum(scores, axis=1, keepdims=True)).T
    hit = chosen[None] == jnp.arange(expert_count, dtype=jnp.int32)[:, None, None]
    dense = jnp.sum(jnp.where(hit, shares[None], 0.0), axis=1)
    tables = [dense] + [along(dense, m) for m in range(1, stages)]

    inside, out_proj = call(
        inside_kernel,
        [((tokens, inner), F32), (out_proj.shape, BF)],
        [pltpu.VMEM(keys.shape, BF)] * 3
        + [pltpu.SemaphoreType.DMA((3, 4)), pltpu.SemaphoreType.DMA],
        away=(0, 1, 2, 3),
    )(queries, keys, values, out_proj, *scalars)

    def ranked(held):
        shape = (len(held) * 2 * groups, tokens)
        body = functools.partial(rank_kernel, groups, length)
        return call(body, [(shape, F32)] * 2)(*scalars[1:], *held)

    own_tables = ranked(tables[:1])
    rest_tables = ranked(tables[1:])
    lookup = {m: (rest_tables, (m - 1) * 2 * groups) for m in range(1, stages)}
    lookup[0] = (own_tables, 0)

    mine = added(*arrived)
    other = swap(mine)
    residual, moe_in, *near = call(
        functools.partial(project_kernel, slots),
        [((tokens, features), BF)] * 2 + [((slots, features), BF)] * (2 * groups),
        [pltpu.VMEM((tokens, inner), BF)],
    )(
        scalars[0],
        inside,
        queries,
        mine,
        other,
        pair,
        lin_gain.reshape(1, inner),
        resid_in.reshape(tokens, features),
        out_proj,
        moe_gain.reshape(1, features),
        own_tables[1],
    )

    routing = sending(stages)
    returning = homing(stages)
    blocks = {0: moe_in}
    outs = {}
    for m in range(1, stages):
        source, shift = routing[m]
        blocks[m] = along(blocks[source], shift)
    for m in range(stages):
        (routes, ranks), base = lookup[m]
        picked = near
        if m:
            picked = select(slots, 2 * groups, base, blocks[m], ranks)
        taken = straight(picked)
        outs[m] = experts(taken, gate_weight, up_weight, down_weight)
    sums = {m: [] for m in range(stages)}
    sums[0].append(residual)
    for m in back_order(stages):
        (routes, ranks), base = lookup[m]
        backs = straight(outs[m])
        part = combine(slots, base, backs, ranks, routes, sums[m], m == 0)
        if m:
            into, shift = returning[m]
            sums[into].append(along(part, shift))
    return part.reshape(1, tokens, features)


def sending(stages):
    if stages == 4:
        return {1: (0, 1), 2: (0, 2), 3: (2, 1)}
    return {m: (0, m) for m in range(1, stages)}


def homing(stages):
    if stages == 4:
        return {2: (3, 1), 3: (0, 3), 1: (0, 1)}
    return {m: (0, m) for m in range(1, stages)}


def back_order(stages):
    return list(range(2, stages)) + [1, 0]


def solution(mesh):
    rows = P("grp", "seq", None)
    held = P(("grp", "seq"), None, None)
    in_specs = (rows, rows, rows, rows, P(), P(), P(), rows, rows, held, held, held)

    return jax.shard_map(on_device, mesh=mesh, in_specs=in_specs, out_specs=rows, check_vma=False)
```
